32 devices in a mesh: dir: 4 (over x, core), tb: 8 (over z, y).
Axes of the slice: x: 2, y: 2, z: 4, core: 2. Of those that a mesh axis runs over, the one named last changes fastest.
Arguments:
- visibilities: bfloat16 [8192, 128], P('tb'), may hold values from -6 to 6
- uv_coords: bfloat16 [2, 8192], P(None, 'tb'), may hold values from -32 to 32
- comp_lm: float32 [2, 12288], P(None, 'dir'), may hold values from -0.25 to 0.25
- spectra: bfloat16 [2, 12288, 128], P(None, 'dir'), may hold values from -0.1875 to 0.1875
- ridge_weight: float32 [128], replicated, may hold values from 32 to 512
- assignment: int32 [12288], P('dir'), may hold values from 0 to 3071, as said below
- peel_order: int32 [12], P('dir'), may hold values from 0 to 2, as said below
- block_tile: int32 [256, 1], P('tb'), may hold values from 0 to 7; in each aligned block of 32 rows (0 to 31, 32 to 63, ...) at most 8 rows name the same one
Outputs:
- residual: bfloat16 [8192, 128], P('tb')
- subgrids: float32 [8, 2, 1024, 128], P('tb', None, 'dir')
The draws below stay inside these ranges and needn't reach their ends.
Inputs may be any that keep to these rules, and one draw needn't show every extreme that they name: `assignment`: each owner's 3 * 1024 entries are a permutation of its local component numbers. `peel_order`: each owner's 3 entries are a permutation of its directions. `block_tile`: among the 32 blocks of one index of tb no tile is named more than 8 times; every tile is named by some block of the whole array.
All inputs are finite; a program needn't handle non-finite values.
Results may differ from the reference program's by a relative error of at most 0.0064.
Values may be sent and summed in bfloat16 or wider, within the bound.
A program may use at most 64 MiB of HBM per device.

```python
import math
import jax
import jax.numpy as jnp
import numpy as np
from jax import lax

COLS = 128
NCOMP = 1024
GRID = 32
DIR_DEV = 3
ITERS = 4
BB = 32
GB = 128
ROWS_DEV = 1024
NB = 32
MOST = 8
SAMPLES = 8192
BLOCKS = 256
TILES = 8
NPOOL = 12288
PIX = 1024
N_DIR = 4


def shuffle_pool(subkey):
    return jax.random.permutation(subkey, DIR_DEV * NCOMP)


def shuffle_order(subkey):
    return jax.random.permutation(subkey, DIR_DEV)


def draw_assignment(key, part):
    subkeys = jax.random.split(jax.random.fold_in(key, 11), N_DIR)
    permuted = jax.vmap(shuffle_pool)(subkeys)
    return permuted.reshape(-1).astype(jnp.int32)


def draw_peel_order(key, part):
    subkeys = jax.random.split(jax.random.fold_in(key, 23), N_DIR)
    permuted = jax.vmap(shuffle_order)(subkeys)
    return permuted.reshape(-1).astype(jnp.int32)


def shard_levels(own_key, dims, cuts, low, largest):
    loudness = 1.0
    for dim, blocks in cuts:
        steps = jax.random.uniform(jax.random.fold_in(jax.random.fold_in(own_key, 6), dim), (blocks,), jnp.float32, low / len(cuts), largest / len(cuts))
        loudness = loudness * jnp.repeat(jnp.exp(steps), dims[dim] // blocks).reshape((-1,) + (1,) * (len(dims) - 1 - dim))
    return loudness


def deal_out(rng, own, number, rows, amount, top, reach, lean):
    ranking = jax.random.permutation(rng, amount)
    crowded, common = portions_of(amount, rows * top, reach, lean, True), portions_of(amount, rows * top, reach, lean, False)
    places = jnp.arange(amount)

    def named(tallies, offset_by):
        used = int((tallies > 0).sum())
        fixed = max(1, used // 4)
        shifted = fixed + (places - fixed + offset_by * (used - fixed)) % max(1, amount - fixed)
        return jnp.zeros((amount,), jnp.int32).at[ranking[jnp.where(places < fixed, places, shifted)]].set(jnp.asarray(tallies, jnp.int32))

    tallies = jnp.where(number % 4 == 0, named(crowded, number // 4), named(common, number - number // 4 - 1))
    mixed = jax.random.permutation(jax.random.fold_in(own, 3), amount)
    donor, receiver = mixed[0:amount // 2 * 2:2], mixed[1:amount // 2 * 2:2]
    room = jnp.minimum(tallies[donor] - 1, reach - tallies[receiver]) // 2
    room = jnp.where((donor == ranking[0]) | (receiver == ranking[0]) | (tallies[receiver] == 0), 0, jnp.maximum(room, 0))
    shifted = jax.random.randint(jax.random.fold_in(own, 4), (amount // 2,), 0, 1 << 20) % (room + 1)
    tallies = tallies.at[donor].add(-shifted).at[receiver].add(shifted)
    labels = jnp.searchsorted(jnp.cumsum(tallies), jnp.arange(rows * top), side="right").astype(jnp.int32)
    listing = labels.reshape(top, rows).T
    listing = listing[jax.random.permutation(jax.random.fold_in(own, 1), rows)]
    offset_by = jax.random.randint(jax.random.fold_in(own, 2), (rows, 1), 0, top)
    return jnp.take_along_axis(listing, (jnp.arange(top)[None, :] + offset_by) % top, axis=1)


def portions_of(number_of, total, bound, lean, full):
    loads = [(1 << 20) // math.isqrt(grade ** lean) + 1 for grade in range(1, number_of + 1)]
    largest = bound if full else min(bound, max(-(-total // number_of), total * loads[0] // sum(loads)))
    least = 1 if total - largest >= number_of - 1 else 0
    given, surplus = [largest] + [least] * (number_of - 1), total - largest - least * (number_of - 1)
    while surplus > 0:
        candidates = [i for i in range(1, number_of) if given[i] < largest] or [i for i in range(1, number_of) if given[i] < bound]
        pool, remaining = sum([loads[i] for i in candidates]), surplus
        for i in candidates:
            more = min(bound - given[i], max(1, remaining * loads[i] // pool), surplus)
            given[i] = given[i] + more
            surplus = surplus - more
    return np.array(given)


def bell_draw(key, dims, scale, most, cuts=(), held_as=jnp.bfloat16):
    loudness = shard_levels(key, dims, cuts, -0.22, 0.18) if cuts else 1.0
    result = jax.random.normal(key, dims, jnp.float32) * scale * loudness
    return jnp.minimum(jnp.maximum(result, -most), most).astype(held_as)


def setup_inputs(seed: int = 0) -> dict:
    arg_keys = jax.random.split(jax.random.key(seed), 9)
    visibilities = bell_draw(arg_keys[0], (SAMPLES, COLS), 1.0, 6.0, ((0, 8),))
    uv_coords = jnp.clip(jax.random.uniform(arg_keys[1], (2, SAMPLES), jnp.float32, -32.0, 32.0) * shard_levels(arg_keys[1], (2, SAMPLES), ((1, 8),), -0.4, 0.0), -32.0, 32.0).astype(jnp.bfloat16)
    comp_lm = jnp.clip(jax.random.uniform(arg_keys[2], (2, NPOOL), jnp.float32, -0.25, 0.25) * shard_levels(arg_keys[2], (2, NPOOL), ((1, 4),), -0.4, 0.0), -0.25, 0.25)
    spectra = bell_draw(arg_keys[3], (2, NPOOL, COLS), NCOMP ** -0.5, 0.1875, ((1, 4),))
    ridge_weight = jnp.clip(jnp.exp(jax.random.uniform(arg_keys[4], (COLS,), jnp.float32, math.log(32.0), math.log(512.0))), 32.0, 512.0)
    assignment = draw_assignment(jax.random.fold_in(arg_keys[8], 71), 0)
    peel_order = draw_peel_order(jax.random.fold_in(arg_keys[8], 71), 0)
    block_tile_keys = jax.random.split(jax.random.fold_in(arg_keys[7], 1), BLOCKS // NB)
    block_tile_turns = jax.random.permutation(jax.random.fold_in(arg_keys[7], 3), BLOCKS // NB)
    block_tile = jax.vmap(lambda own, number: deal_out(jax.random.fold_in(arg_keys[7], 2), own, number, NB, TILES, 1, MOST, 2))(block_tile_keys, block_tile_turns).reshape((BLOCKS, 1))
    return {"visibilities": visibilities, "uv_coords": uv_coords, "comp_lm": comp_lm, "spectra": spectra, "ridge_weight": ridge_weight, "assignment": assignment, "peel_order": peel_order, "block_tile": block_tile}


TWO_PI = 2.0 * math.pi


def phase_table(coords, lm_dir):
    phases = TWO_PI * (coords[0][:, None] * lm_dir[0][None, :] + coords[1][:, None] * lm_dir[1][None, :])
    return jnp.concatenate([jnp.cos(phases), jnp.sin(phases)], axis=1).astype(jnp.bfloat16)


def predict(coords, lm_dir, spec_dir):
    phase_rows = phase_table(coords, lm_dir)
    return jnp.dot(phase_rows, spec_dir.reshape(-1, spec_dir.shape[-1]), preferred_element_type=jnp.float32)


def neighbours(gain_values):
    blocks, columns = gain_values.shape
    paired = gain_values.reshape(blocks, columns // 2, 2)
    padded = jnp.pad(paired, ((0, 0), (1, 1), (0, 0)), mode="edge")
    return (0.5 * (padded[:, :-2] + padded[:, 2:])).reshape(blocks, columns)


def fit_subtract(remains, model_rows, ridge_weight):
    blocks = remains.shape[0] // GB
    res_blocks = remains.reshape(blocks, GB, -1)
    mod_blocks = model_rows.reshape(blocks, GB, -1)
    cross_sum = jnp.sum(res_blocks * mod_blocks, axis=1)
    power_sum = jnp.sum(mod_blocks * mod_blocks, axis=1)
    gain_values = jnp.ones_like(cross_sum)
    for sweep_index in range(ITERS):
        gain_values = (cross_sum + ridge_weight * neighbours(gain_values)) / (power_sum + ridge_weight)
    return (res_blocks - gain_values[:, None, :] * mod_blocks).reshape(remains.shape)


def grid_table(coords, x_pixel, y_pixel):
    phases = TWO_PI * (coords[0][:, None] * x_pixel[None, :] + coords[1][:, None] * y_pixel[None, :]) / (2.0 * GRID)
    return jnp.cos(phases).astype(jnp.bfloat16), jnp.sin(phases).astype(jnp.bfloat16)


def reference(visibilities, uv_coords, comp_lm, spectra, ridge_weight, assignment, peel_order, block_tile):
    columns = visibilities.shape[1]
    ndirs = peel_order.shape[0]
    pool_owner = DIR_DEV * NCOMP
    groups = visibilities.shape[0] // ROWS_DEV

    def one_group(group_index):
        first_row = group_index * ROWS_DEV
        remains = lax.dynamic_slice_in_dim(visibilities, first_row, ROWS_DEV, 0).astype(jnp.float32)
        coords = lax.dynamic_slice_in_dim(uv_coords, first_row, ROWS_DEV, 1).astype(jnp.float32)
        rounded = remains.astype(jnp.bfloat16)
        for position in range(ndirs):
            owner_base = (position // DIR_DEV) * pool_owner
            first_entry = owner_base + peel_order[position] * NCOMP
            chosen = owner_base + lax.dynamic_slice_in_dim(assignment, first_entry, NCOMP, 0)
            model_rows = predict(coords, comp_lm[:, chosen], spectra[:, chosen])
            remains = fit_subtract(remains, model_rows, ridge_weight)
            if (position + 1) % DIR_DEV == 0:
                rounded = lax.optimization_barrier(remains.astype(jnp.bfloat16))
                remains = rounded.astype(jnp.float32)
        return rounded

    residual = lax.map(one_group, jnp.arange(groups, dtype=jnp.int32)).reshape(-1, columns)
    pixels = jnp.arange(PIX, dtype=jnp.int32)
    x_pixel = (pixels // GRID - GRID // 2).astype(jnp.float32)
    y_pixel = (pixels % GRID - GRID // 2).astype(jnp.float32)
    blocks = residual.reshape(-1, BB, columns)
    block_coords = uv_coords.astype(jnp.float32).reshape(2, -1, BB).transpose(1, 0, 2)
    contract = (((0,), (0,)), ((), ()))

    def add_block(subgrids, block_items):
        block_rows, coords, tile_index = block_items
        cos_table, sin_table = grid_table(coords, x_pixel, y_pixel)
        real_part = lax.dot_general(cos_table, block_rows, contract, preferred_element_type=jnp.float32)
        imag_part = lax.dot_general(sin_table, block_rows, contract, preferred_element_type=jnp.float32)
        update = jnp.stack([real_part, imag_part])
        return subgrids.at[tile_index].add(update), None

    initial = jnp.zeros((TILES, 2, PIX, columns), jnp.float32)
    subgrids, unused = lax.scan(add_block, initial, (blocks, block_coords, block_tile[:, 0]))
    return residual, subgrids * (float(ROWS_DEV) ** -0.5)
```

```python
import functools
import math

import jax
import jax.numpy as jnp
from jax import lax
from jax.experimental import pallas as pl
from jax.experimental.pallas import tpu as pltpu
from jax.sharding import PartitionSpec as P

NCOMP = 1024
GRID = 32
DIR_DEV = 3
ITERS = 4
BB = 32
GB = 128
ROWS_DEV = 1024
PIX = 1024

MESH = pl.DeviceIdType.MESH
F32 = jnp.float32
BF16 = jnp.bfloat16
LANES = 128
CHUNK = 256
SUB = 32

SIN_FIT = (4.4428795675460835, -7.307816684491791, 3.5977741780872416, -0.7911993921613704)
COS_FIT = (1.414204014809076, -6.977637323456295, 5.715187874756718, -1.728213892223522)


def horner(square, fit):
    total = fit[-1]
    for coefficient in fit[-2::-1]:
        total = total * square + coefficient
    return total


def turn_cos_sin(turns):
    part = turns - jnp.round(turns)
    square = part * part
    half_sin = part * horner(square, SIN_FIT)
    half_cos = horner(square, COS_FIT)
    return 1.0 - half_sin * half_sin, half_sin * half_cos


def kernel(
    owners,
    peers,
    slots,
    uv_ref,
    lm_ref,
    ridge_ref,
    entry_ref,
    tile_ref,
    peel_ref,
    vis_hbm,
    spec_hbm,
    resid_ref,
    grid_ref,
    vis_buf,
    spec_buf,
    masked,
    lm_parts,
    coord_rows,
    block_row,
    block_of_ref,
    coords_out,
    turned_a,
    turned_b,
    acc,
    models_out,
    models_in,
    resid,
    own_rows,
    rows_out,
    rows_in,
    coords_in,
    tables,
    m_send,
    m_recv,
    r_send,
    r_recv,
    d_send,
    d_recv,
    f_send,
    f_recv,
    c_send,
    c_recv,
    local_sem,
):
    me_d = lax.axis_index("dir")
    me_t = lax.axis_index("tb")
    core = me_d % 2
    partner = me_d + 1 - 2 * core
    group_rows, columns = vis_buf.shape
    sample_rows = group_rows * owners
    comps = lm_ref.shape[1]
    block_count = sample_rows // BB
    group_blocks = block_count // owners
    slot_rows = slots * BB
    half_slots = slots // 2
    half_rows = half_slots * BB
    first = me_d * group_rows

    spec_copy = pltpu.make_async_copy(spec_hbm, spec_buf, local_sem.at[0])
    vis_copy = pltpu.make_async_copy(
        vis_hbm.at[pl.ds(pl.multiple_of(first, group_rows), group_rows)], vis_buf, local_sem.at[1]
    )
    spec_copy.start()
    vis_copy.start()

    barrier = pltpu.get_barrier_semaphore()
    for k in range(1, owners):
        pl.semaphore_signal(
            barrier, inc=1, device_id={"dir": lax.rem(me_d + k, owners)}, device_id_type=MESH
        )

    def greet(k, carry):
        pl.semaphore_signal(
            barrier, inc=1, device_id={"tb": lax.rem(me_t + k, peers)}, device_id_type=MESH
        )
        return carry

    lax.fori_loop(1, peers, greet, 0)

    slot_lanes = block_row.shape[1]
    tiles = jnp.broadcast_to(tile_ref[...], (slot_lanes, block_count))
    named_tile = jnp.where(
        lax.broadcasted_iota(jnp.int32, (slot_lanes, block_count), 0) == tiles, 1.0, 0.0
    )
    earlier = jnp.where(
        lax.broadcasted_iota(jnp.int32, (block_count, block_count), 0)
        < lax.broadcasted_iota(jnp.int32, (block_count, block_count), 1),
        1.0,
        0.0,
    )
    ranks = jnp.dot(named_tile.astype(BF16), earlier.astype(BF16), preferred_element_type=F32)
    slot = jnp.sum(ranks * named_tile, axis=0, keepdims=True).astype(jnp.int32)
    target = jnp.broadcast_to(tile_ref[...] * slots + slot, (slot_lanes, block_count))
    lane = lax.broadcasted_iota(jnp.int32, (slot_lanes, block_count), 0)
    taken = jnp.where(lane == target, 1.0, 0.0).astype(BF16)
    block_id = lax.broadcasted_iota(jnp.int32, (8, block_count), 1) - block_count
    picked = lax.dot_general(
        block_id.astype(F32).astype(BF16),
        taken,
        (((1,), (1,)), ((), ())),
        preferred_element_type=F32,
    )
    block_row[...] = picked[0:1, :].astype(jnp.int32) + block_count
    index_copy = pltpu.make_async_copy(block_row, block_of_ref, local_sem.at[2])
    index_copy.start()

    u_row = uv_ref[0:1, :].astype(F32)
    v_row = uv_ref[1:2, :].astype(F32)
    in_block = (
        lax.broadcasted_iota(jnp.int32, (block_count, sample_rows), 1) // BB
        == lax.broadcasted_iota(jnp.int32, (block_count, sample_rows), 0)
    )
    at_lane = jnp.where(
        lax.broadcasted_iota(jnp.int32, (sample_rows, LANES), 0) % BB
        == lax.broadcasted_iota(jnp.int32, (sample_rows, LANES), 1) % BB,
        1.0,
        0.0,
    ).astype(BF16)
    packed, side = coords_out.shape[1], coords_out.shape[1] // 2
    spot = lax.broadcasted_iota(jnp.int32, (peers * packed, block_count), 0)
    place_of = tile_ref[...] * packed + slot
    sent = jnp.zeros((peers * packed, LANES), F32)
    for which, row in enumerate((u_row, v_row)):
        spread = jnp.where(in_block, jnp.broadcast_to(row, in_block.shape), 0.0).astype(BF16)
        by_block = jnp.dot(spread, at_lane, preferred_element_type=F32).astype(BF16)
        chosen = jnp.where(spot == place_of + which * side, 1.0, 0.0).astype(BF16)
        sent = sent + jnp.dot(chosen, by_block, preferred_element_type=F32)
    coords_out[...] = sent.astype(BF16).reshape(peers, packed, LANES)

    stacked = jnp.concatenate(
        [u_row] * 3 + [v_row] * 3 + [jnp.zeros((LANES - 6, sample_rows), F32)], axis=0
    )
    coord_rows[...] = stacked.T.astype(BF16)

    parts = []
    for which in range(2):
        left = lm_ref[which : which + 1, :]
        for part in range(3):
            rounded = left.astype(BF16).astype(F32)
            parts.append(rounded)
            left = left - rounded
    parts.append(jnp.zeros((2, comps), F32))
    lm_parts[...] = jnp.concatenate(parts, axis=0).astype(BF16)

    strips = comps // LANES
    padded = -(-strips // 16) * 16
    named = jnp.concatenate([entry_ref[r : r + 1, :] for r in range(strips)], axis=1)
    places = []
    for direction in range(DIR_DEV):
        value = jnp.int32(0)
        for position in range(DIR_DEV):
            value = value + jnp.where(peel_ref[position] == direction, position, 0)
        places.append(jnp.full((1, comps // DIR_DEV), value, jnp.int32))
    place = jnp.concatenate(places, axis=1).astype(F32)
    low = lax.broadcasted_iota(jnp.int32, (LANES, comps), 0)
    high = lax.broadcasted_iota(jnp.int32, (padded, comps), 0)
    at_low = jnp.where(low == named % LANES, 1.0, 0.0).astype(BF16)
    at_high = jnp.where(high == named // LANES, place, 0.0).astype(BF16)
    positions = lax.dot_general(
        at_low, at_high, (((1,), (1,)), ((), ())), preferred_element_type=F32
    )
    spec_copy.wait()
    for strip in range(strips):
        own = jnp.broadcast_to(positions[:, strip : strip + 1], (LANES, columns)).astype(BF16)
        span = pl.ds(strip * LANES, LANES)
        for part in range(2):
            values = spec_buf[part, span, :]
            for position in range(DIR_DEV):
                masked[part, span, position * columns : (position + 1) * columns] = jnp.where(
                    own == jnp.asarray(position, BF16), values, jnp.zeros_like(values)
                )

    def coords_copy(src, owner, to):
        return pltpu.make_async_remote_copy(
            src_ref=coords_out.at[src],
            dst_ref=coords_in.at[owner],
            send_sem=c_send.at[src],
            recv_sem=c_recv.at[owner],
            device_id={"tb": to},
            device_id_type=MESH,
        )

    def models_copy(group, owner, to):
        return pltpu.make_async_remote_copy(
            src_ref=models_out.at[group],
            dst_ref=models_in.at[owner],
            send_sem=m_send.at[group],
            recv_sem=m_recv.at[owner],
            device_id={"dir": to},
            device_id_type=MESH,
        )

    def nth_group(k):
        far = jnp.where(k < owners // 2, k + owners // 2, owners - 1 - k)
        return lax.rem(me_d // 2 + far // 2, owners // 2) * 2 + lax.rem(me_d + far, 2)

    def send_coords(k, carry):
        to = lax.rem(me_t + k, peers)
        coords_copy(to, me_t, to).start()
        return carry

    def predict_group(k, carry):
        group = nth_group(k)
        group_coords = coord_rows[
            pl.ds(pl.multiple_of(group * group_rows, group_rows), group_rows), 0:8
        ]
        chunks = comps // CHUNK
        buffers = (turned_a, turned_b)
        pieces = group_rows // SUB

        def spread_turns(chunk):
            return jnp.dot(
                group_coords,
                lm_parts[:, chunk * CHUNK : (chunk + 1) * CHUNK],
                preferred_element_type=F32,
            )

        def contract_chunk(chunk, part):
            return jnp.dot(
                buffers[chunk % 2][part],
                masked[part, chunk * CHUNK : (chunk + 1) * CHUNK, :],
                preferred_element_type=F32,
            )

        turns = spread_turns(0)
        for chunk in range(chunks):
            turned = buffers[chunk % 2]
            following = None
            for sub in range(pieces):
                rows = slice(sub * SUB, (sub + 1) * SUB)
                cos_part, sin_part = turn_cos_sin(turns[rows])
                turned[0, rows, :] = cos_part.astype(BF16)
                turned[1, rows, :] = sin_part.astype(BF16)
                if chunk > 0 and sub == 0:
                    update = contract_chunk(chunk - 1, 0)
                if chunk > 0 and sub == pieces // 2 - 1:
                    update = update + contract_chunk(chunk - 1, 1)
                    if chunk == 1:
                        acc[...] = update
                    else:
                        acc[...] += update
                if chunk + 1 < chunks and sub == pieces - 2:
                    following = spread_turns(chunk + 1)
            turns = following
        last = contract_chunk(chunks - 1, 0) + contract_chunk(chunks - 1, 1)
        final = (acc[...] + last).astype(BF16)

        @pl.when(k == 0)
        def _():
            pl.semaphore_wait(barrier, owners - 1 + peers - 1)

        @pl.when(k < owners - 1)
        def _():
            models_out[group] = final
            models_copy(group, me_d, group).start()

        @pl.when(k == 0)
        def _():
            lax.fori_loop(1, peers, send_coords, 0)

        @pl.when(k == owners - 1)
        def _():
            models_in[me_d] = final

        return carry

    lax.fori_loop(0, owners, predict_group, 0)
    coords_in[me_t] = coords_out[me_t]
    index_copy.wait()
    vis_copy.wait()

    def wait_models(k, carry):
        source = nth_group(k)
        models_copy(source, source, source).wait()
        return carry

    lax.fori_loop(0, owners - 1, wait_models, 0)

    gain_blocks = group_rows // GB
    ridge = jnp.broadcast_to(ridge_ref[...], (8, columns))
    lane = lax.broadcasted_iota(jnp.int32, (8, columns), 1)
    stripe = lax.broadcasted_iota(jnp.int32, (8, columns), 0) // (8 // gain_blocks)
    reach = 2 * (ITERS - 1)

    def side_by_side(values):
        total = None
        for block in range(gain_blocks):
            part = jnp.sum(jnp.sum(values[block], axis=0), axis=0, keepdims=True)
            part = jnp.broadcast_to(part, (8, columns))
            total = part if block == 0 else jnp.where(stripe == block, part, total)
        return total

    def of_block(value, block):
        row = block * (8 // gain_blocks)
        return jnp.broadcast_to(value[row : row + 1, :], (8, columns))[None]

    def moved(value, far):
        rolled = {0: value}
        for shift in range(2, far + 1, 2):
            rolled[shift] = pltpu.roll(value, columns - shift, 1)
            rolled[-shift] = pltpu.roll(value, shift, 1)
        out = {0: value}
        for shift in range(2, far + 1, 2):
            right, left = rolled[shift], rolled[-shift]
            for step in range(shift // 2):
                mirror = shift - 2 - 4 * step
                left = jnp.where(lane // 2 == step, rolled[mirror], left)
                right = jnp.where(lane // 2 == columns // 2 - 1 - step, rolled[-mirror], right)
            out[shift], out[-shift] = right, left
        return out

    def sweep_gain(constant, couple):
        base = moved(constant, reach)
        gain = {shift: base[shift] + 2.0 * couple[shift] for shift in base}
        for sweep in range(1, ITERS):
            far = reach - 2 * sweep
            gain = {
                shift: base[shift] + couple[shift] * (gain[shift - 2] + gain[shift + 2])
                for shift in range(-far, far + 1, 2)
            }
        return gain[0]

    rest = [
        vis_buf[block * GB : (block + 1) * GB, :].astype(F32).reshape(GB // 8, 8, columns)
        for block in range(gain_blocks)
    ]

    def peel_owner(owner, rest):
        models = [
            [
                models_in[
                    owner,
                    block * GB : (block + 1) * GB,
                    position * columns : (position + 1) * columns,
                ]
                .astype(F32)
                .reshape(GB // 8, 8, columns)
                for block in range(gain_blocks)
            ]
            for position in range(DIR_DEV)
        ]
        every = range(gain_blocks)
        gains = []
        for position in range(DIR_DEV):
            model = models[position]
            inverse = 1.0 / (side_by_side([model[b] * model[b] for b in every]) + ridge)
            couple = moved(0.5 * ridge * inverse, reach)
            cross_sum = side_by_side([rest[b] * model[b] for b in every])
            for earlier_one in range(position):
                other = models[earlier_one]
                shared = side_by_side([other[b] * model[b] for b in every])
                cross_sum = cross_sum - gains[earlier_one] * shared
            gains.append(sweep_gain(cross_sum * inverse, couple))
        out = []
        for b in every:
            left = rest[b]
            for position in range(DIR_DEV):
                left = left - of_block(gains[position], b) * models[position][b]
            out.append(left.astype(BF16).astype(F32))
        return tuple(out)

    done = lax.fori_loop(0, owners, peel_owner, tuple(rest))
    per_gain = GB // BB
    for block in range(gain_blocks):
        resid[pl.ds(me_d * group_blocks + block * per_gain, per_gain)] = (
            done[block].reshape(per_gain, BB, columns).astype(BF16)
        )
    resid[block_count] = jnp.zeros((BB, columns), BF16)

    def resid_copy(group, sem, to):
        part = pl.ds(group * group_blocks, group_blocks)
        return pltpu.make_async_remote_copy(
            src_ref=resid.at[part],
            dst_ref=resid.at[part],
            send_sem=r_send.at[sem],
            recv_sem=r_recv.at[group],
            device_id={"dir": to},
            device_id_type=MESH,
        )

    for k in range(1, owners):
        to = lax.rem(me_d + k, owners)
        resid_copy(me_d, to, to).start()
    for k in range(1, owners):
        source = lax.rem(me_d + k, owners)
        resid_copy(source, source, source).wait_recv()

    def block_in(to, slot):
        block = block_of_ref[0, to * slots + slot]
        return jnp.minimum(jnp.maximum(block, 0), block_count)

    def half_of(which):
        return pl.ds(pl.multiple_of(which * half_rows, half_rows), half_rows)

    def rows_copy(src, owner, to):
        return pltpu.make_async_remote_copy(
            src_ref=rows_out.at[src],
            dst_ref=rows_in.at[owner, half_of(core)],
            send_sem=d_send.at[src],
            recv_sem=d_recv.at[owner],
            device_id={"tb": to},
            device_id_type=MESH,
        )

    def hand_over(owner, which):
        return pltpu.make_async_remote_copy(
            src_ref=rows_in.at[owner, half_of(which)],
            dst_ref=rows_in.at[owner, half_of(which)],
            send_sem=f_send.at[owner],
            recv_sem=f_recv.at[owner],
            device_id={"dir": partner},
            device_id_type=MESH,
        )

    def dispatch(k, carry):
        to = lax.rem(me_t + k, peers)
        for slot in range(half_slots):
            rows_out[to, slot * BB : (slot + 1) * BB, :] = resid[
                block_in(to, core * half_slots + slot)
            ]
        rows_copy(to, me_t, to).start()
        return carry

    lax.fori_loop(1, peers, dispatch, 0)
    for slot in range(slots):
        own_rows[slot * BB : (slot + 1) * BB, :] = resid[block_in(me_t, slot)]
    resid_ref[...] = resid[0:block_count].reshape(sample_rows, columns)

    def wait_coords(k, carry):
        source = lax.rem(me_t + k, peers)
        coords_copy(source, source, source).wait()
        return carry

    lax.fori_loop(1, peers, wait_coords, 0)
    share = grid_ref.shape[1]
    lines = share // GRID
    slots_wide = LANES // BB
    strips_wide = -(-slot_rows // LANES)
    wide = strips_wide * LANES
    x_of = (
        me_d * lines - GRID // 2 + lax.broadcasted_iota(jnp.int32, (lines, wide), 0)
    ).astype(F32) / (2.0 * GRID)
    y_of = (lax.broadcasted_iota(jnp.int32, (GRID, wide), 0) - GRID // 2).astype(F32) / (
        2.0 * GRID
    )
    slot_at = lax.broadcasted_iota(jnp.int32, (side, LANES), 0)
    slot_for = lax.broadcasted_iota(jnp.int32, (side, LANES), 1) // BB

    def make_table(source, carry):
        given = coords_in[source].astype(F32)

        def flat(rows):
            return jnp.concatenate(
                [
                    jnp.sum(
                        jnp.where(slot_at == slot_for + strip * slots_wide, rows, 0.0),
                        axis=0,
                        keepdims=True,
                    )
                    for strip in range(strips_wide)
                ],
                axis=1,
            )

        cos_x, sin_x = turn_cos_sin(x_of * flat(given[0:side]))
        cos_y, sin_y = turn_cos_sin(y_of * flat(given[side:packed]))
        for line in range(lines):
            cos_l, sin_l = cos_x[line : line + 1], sin_x[line : line + 1]
            rows = slice(line * GRID, (line + 1) * GRID)
            lower = slice(share + line * GRID, share + (line + 1) * GRID)
            cos_part = (cos_l * cos_y - sin_l * sin_y).astype(BF16)
            sin_part = (sin_l * cos_y + cos_l * sin_y).astype(BF16)
            tables[source, rows, :] = cos_part[:, 0:slot_rows]
            tables[source, lower, :] = sin_part[:, 0:slot_rows]
        return carry

    lax.fori_loop(0, peers, make_table, 0)

    grid_sum = jnp.dot(tables[me_t], own_rows[...], preferred_element_type=F32)

    def source_at(k):
        return lax.rem(me_t + peers - k, peers)

    def arrive(k):
        source = source_at(k)
        rows_copy(source, source, source).wait_recv()
        hand_over(source, core).start()

    def add_source(k, total):
        @pl.when(k + 1 < peers)
        def _():
            arrive(k + 1)

        source = source_at(k)
        hand_over(source, 1 - core).wait_recv()
        return total + jnp.dot(tables[source], rows_in[source], preferred_element_type=F32)

    arrive(1)
    grid_sum = lax.fori_loop(1, peers, add_source, grid_sum)
    grid_ref[...] = (grid_sum * float(ROWS_DEV) ** (-0.5)).reshape(2, share, columns)

    for k in range(1, owners):
        to = lax.rem(me_d + k, owners)
        resid_copy(me_d, to, to).wait_send()

    def drain(k, carry):
        to = lax.rem(me_t + k, peers)
        rows_copy(to, me_t, to).wait_send()
        hand_over(to, core).wait_send()
        return carry

    lax.fori_loop(1, peers, drain, 0)


def finish(resid_ref, grid_ref, resid_out, grid_out, sem):
    copies = (
        pltpu.make_async_copy(resid_ref, resid_out, sem.at[0]),
        pltpu.make_async_copy(grid_ref, grid_out, sem.at[1]),
    )
    for copy in copies:
        copy.start()
    for copy in copies:
        copy.wait()


def local(
    owners,
    peers,
    visibilities,
    uv_coords,
    comp_lm,
    spectra,
    ridge_weight,
    assignment,
    peel_order,
    block_tile,
):
    sample_rows, columns = visibilities.shape
    comps = comp_lm.shape[1]
    block_count = sample_rows // BB
    slots = max(2, 2 * block_count // peers)
    share = PIX // owners

    slot_lanes = -(-peers * slots // LANES) * LANES
    packed = 16 * -(-slots // 8)
    group_rows = sample_rows // owners
    half_rows = slots // 2 * BB
    vmem = pl.BlockSpec(memory_space=pltpu.VMEM)
    smem = pl.BlockSpec(memory_space=pltpu.SMEM)
    anywhere = pl.BlockSpec(memory_space=pl.ANY)
    dma = pltpu.SemaphoreType.DMA
    residual, subgrid = pl.pallas_call(
        functools.partial(kernel, owners, peers, slots),
        out_shape=(
            jax.ShapeDtypeStruct((sample_rows, columns), BF16),
            jax.ShapeDtypeStruct((2, share, columns), F32),
        ),
        in_specs=[vmem] * 5 + [smem] + [anywhere] * 2,
        out_specs=(vmem, vmem),
        scratch_shapes=[
            pltpu.VMEM((group_rows, columns), BF16),
            pltpu.VMEM((2, comps, columns), BF16),
            pltpu.VMEM((2, comps, DIR_DEV * columns), BF16),
            pltpu.VMEM((8, comps), BF16),
            pltpu.VMEM((sample_rows, LANES), BF16),
            pltpu.VMEM((1, slot_lanes), jnp.int32),
            pltpu.SMEM((1, slot_lanes), jnp.int32),
            pltpu.VMEM((peers, packed, LANES), BF16),
            pltpu.VMEM((2, group_rows, CHUNK), BF16),
            pltpu.VMEM((2, group_rows, CHUNK), BF16),
            pltpu.VMEM((group_rows, DIR_DEV * columns), F32),
            pltpu.VMEM((owners, group_rows, DIR_DEV * columns), BF16),
            pltpu.VMEM((owners, group_rows, DIR_DEV * columns), BF16),
            pltpu.VMEM((block_count + 1, BB, columns), BF16),
            pltpu.VMEM((slots * BB, columns), BF16),
            pltpu.VMEM((peers, half_rows, columns), BF16),
            pltpu.VMEM((peers, slots * BB, columns), BF16),
            pltpu.VMEM((peers, packed, LANES), BF16),
            pltpu.VMEM((peers, 2 * share, slots * BB), BF16),
            dma((owners,)),
            dma((owners,)),
            dma((owners,)),
            dma((owners,)),
            dma((peers,)),
            dma((peers,)),
            dma((peers,)),
            dma((peers,)),
            dma((peers,)),
            dma((peers,)),
            dma((3,)),
        ],
        compiler_params=pltpu.CompilerParams(
            collective_id=0, has_side_effects=True, vmem_limit_bytes=60 * 1024 * 1024
        ),
    )(
        uv_coords,
        comp_lm,
        ridge_weight[None, :],
        assignment.reshape(comps // LANES, LANES),
        block_tile.reshape(1, block_count),
        peel_order,
        visibilities,
        spectra,
    )
    residual, subgrid = pl.pallas_call(
        finish,
        out_shape=(
            jax.ShapeDtypeStruct(residual.shape, residual.dtype),
            jax.ShapeDtypeStruct(subgrid.shape, subgrid.dtype),
        ),
        in_specs=[vmem] * 2,
        out_specs=(anywhere, anywhere),
        scratch_shapes=[dma((2,))],
    )(residual, subgrid)
    return residual, subgrid[None]


def solution(mesh):
    return jax.shard_map(
        functools.partial(local, mesh.shape["dir"], mesh.shape["tb"]),
        mesh=mesh,
        in_specs=(
            P("tb", None),
            P(None, "tb"),
            P(None, "dir"),
            P(None, "dir", None),
            P(),
            P("dir"),
            P("dir"),
            P("tb", None),
        ),
        out_specs=(P("tb", None), P("tb", None, "dir", None)),
        check_vma=False,
    )
```

```python
import functools
import math

import jax
import jax.numpy as jnp
from jax import lax
from jax.experimental import pallas as pl
from jax.experimental.pallas import tpu as pltpu
from jax.sharding import PartitionSpec as P

NCOMP = 1024
GRID = 32
DIR_DEV = 3
ITERS = 4
BB = 32
GB = 128
ROWS_DEV = 1024
PIX = 1024

MESH = pl.DeviceIdType.MESH
F32 = jnp.float32
BF16 = jnp.bfloat16
LANES = 128
CHUNK = 256
SUB = 32

SIN_FIT = (4.4428795675460835, -7.307816684491791, 3.5977741780872416, -0.7911993921613704)
COS_FIT = (1.414204014809076, -6.977637323456295, 5.715187874756718, -1.728213892223522)


BENT_SIN = (6.28125, -41.25, 76.5)
BENT_COS = (1.0, -19.75, 65.0, -79.5)


def horner(square, fit):
    total = jnp.asarray(fit[-1], square.dtype)
    for coefficient in fit[-2::-1]:
        total = total * square + jnp.asarray(coefficient, square.dtype)
    return total


def turn_cos_sin(turns):
    part = turns - jnp.round(turns)
    square = part * part
    half_sin = part * horner(square, SIN_FIT)
    half_cos = horner(square, COS_FIT)
    return 1.0 - half_sin * half_sin, half_sin * half_cos


def turn_cos_sin_short(turns):
    part = turns - jnp.round(turns)
    bent = (0.25 - jnp.abs(part)).astype(BF16)
    square = bent * bent
    upright = horner(square, BENT_COS)
    flipped = jnp.where(part.astype(BF16) < 0, -upright, upright)
    return bent * horner(square, BENT_SIN), flipped


def kernel(
    owners,
    peers,
    slots,
    uv_ref,
    lm_ref,
    ridge_ref,
    entry_ref,
    tile_ref,
    peel_ref,
    vis_hbm,
    spec_hbm,
    resid_ref,
    grid_ref,
    vis_buf,
    spec_buf,
    masked,
    lm_parts,
    coord_rows,
    block_row,
    block_of_ref,
    coords_out,
    turned_a,
    turned_b,
    acc,
    models_out,
    models_in,
    resid,
    own_rows,
    rows_out,
    rows_in,
    coords_in,
    tables,
    m_send,
    m_recv,
    r_send,
    r_recv,
    d_send,
    d_recv,
    f_send,
    f_recv,
    c_send,
    c_recv,
    local_sem,
):
    me_d = lax.axis_index("dir")
    me_t = lax.axis_index("tb")
    core = me_d % 2
    partner = me_d + 1 - 2 * core
    group_rows, columns = vis_buf.shape
    sample_rows = group_rows * owners
    comps = lm_ref.shape[1]
    block_count = sample_rows // BB
    group_blocks = block_count // owners
    slot_rows = slots * BB
    half_slots = slots // 2
    half_rows = half_slots * BB
    first = me_d * group_rows

    spec_copy = pltpu.make_async_copy(spec_hbm, spec_buf, local_sem.at[0])
    vis_copy = pltpu.make_async_copy(
        vis_hbm.at[pl.ds(pl.multiple_of(first, group_rows), group_rows)], vis_buf, local_sem.at[1]
    )
    spec_copy.start()
    vis_copy.start()

    barrier = pltpu.get_barrier_semaphore()
    for k in range(1, owners):
        pl.semaphore_signal(
            barrier, inc=1, device_id={"dir": lax.rem(me_d + k, owners)}, device_id_type=MESH
        )

    def greet(k, carry):
        pl.semaphore_signal(
            barrier, inc=1, device_id={"tb": lax.rem(me_t + k, peers)}, device_id_type=MESH
        )
        return carry

    lax.fori_loop(1, peers, greet, 0)

    slot_lanes = block_row.shape[1]
    tiles = jnp.broadcast_to(tile_ref[...], (slot_lanes, block_count))
    named_tile = jnp.where(
        lax.broadcasted_iota(jnp.int32, (slot_lanes, block_count), 0) == tiles, 1.0, 0.0
    )
    earlier = jnp.where(
        lax.broadcasted_iota(jnp.int32, (block_count, block_count), 0)
        < lax.broadcasted_iota(jnp.int32, (block_count, block_count), 1),
        1.0,
        0.0,
    )
    ranks = jnp.dot(named_tile.astype(BF16), earlier.astype(BF16), preferred_element_type=F32)
    slot = jnp.sum(ranks * named_tile, axis=0, keepdims=True).astype(jnp.int32)
    target = jnp.broadcast_to(tile_ref[...] * slots + slot, (slot_lanes, block_count))
    lane = lax.broadcasted_iota(jnp.int32, (slot_lanes, block_count), 0)
    taken = jnp.where(lane == target, 1.0, 0.0).astype(BF16)
    block_id = lax.broadcasted_iota(jnp.int32, (8, block_count), 1) - block_count
    picked = lax.dot_general(
        block_id.astype(F32).astype(BF16),
        taken,
        (((1,), (1,)), ((), ())),
        preferred_element_type=F32,
    )
    block_row[...] = picked[0:1, :].astype(jnp.int32) + block_count
    index_copy = pltpu.make_async_copy(block_row, block_of_ref, local_sem.at[2])
    index_copy.start()

    u_row = uv_ref[0:1, :].astype(F32)
    v_row = uv_ref[1:2, :].astype(F32)
    in_block = (
        lax.broadcasted_iota(jnp.int32, (block_count, sample_rows), 1) // BB
        == lax.broadcasted_iota(jnp.int32, (block_count, sample_rows), 0)
    )
    at_lane = jnp.where(
        lax.broadcasted_iota(jnp.int32, (sample_rows, LANES), 0) % BB
        == lax.broadcasted_iota(jnp.int32, (sample_rows, LANES), 1) % BB,
        1.0,
        0.0,
    ).astype(BF16)
    packed, side = coords_out.shape[1], coords_out.shape[1] // 2
    spot = lax.broadcasted_iota(jnp.int32, (peers * packed, block_count), 0)
    place_of = tile_ref[...] * packed + slot
    sent = jnp.zeros((peers * packed, LANES), F32)
    for which, row in enumerate((u_row, v_row)):
        spread = jnp.where(in_block, jnp.broadcast_to(row, in_block.shape), 0.0).astype(BF16)
        by_block = jnp.dot(spread, at_lane, preferred_element_type=F32).astype(BF16)
        chosen = jnp.where(spot == place_of + which * side, 1.0, 0.0).astype(BF16)
        sent = sent + jnp.dot(chosen, by_block, preferred_element_type=F32)
    coords_out[...] = sent.astype(BF16).reshape(peers, packed, LANES)

    stacked = jnp.concatenate(
        [u_row] * 3 + [v_row] * 3 + [jnp.zeros((2, sample_rows), F32)], axis=0
    )
    coord_rows[...] = stacked.T.astype(BF16)

    parts = []
    for which in range(2):
        left = lm_ref[which : which + 1, :]
        for part in range(3):
            rounded = left.astype(BF16).astype(F32)
            parts.append(rounded)
            left = left - rounded
    parts.append(jnp.zeros((2, comps), F32))
    lm_parts[...] = jnp.concatenate(parts, axis=0).astype(BF16)

    strips = comps // LANES
    padded = -(-strips // 16) * 16
    named = jnp.concatenate([entry_ref[r : r + 1, :] for r in range(strips)], axis=1)
    places = []
    for direction in range(DIR_DEV):
        value = jnp.int32(0)
        for position in range(DIR_DEV):
            value = value + jnp.where(peel_ref[position] == direction, position, 0)
        places.append(jnp.full((1, comps // DIR_DEV), value, jnp.int32))
    place = jnp.concatenate(places, axis=1).astype(F32)
    low = lax.broadcasted_iota(jnp.int32, (LANES, comps), 0)
    high = lax.broadcasted_iota(jnp.int32, (padded, comps), 0)
    at_low = jnp.where(low == named % LANES, 1.0, 0.0).astype(BF16)
    at_high = jnp.where(high == named // LANES, place, 0.0).astype(BF16)
    positions = lax.dot_general(
        at_low, at_high, (((1,), (1,)), ((), ())), preferred_element_type=F32
    )
    spec_copy.wait()
    for strip in range(strips):
        own = jnp.broadcast_to(positions[:, strip : strip + 1], (LANES, columns)).astype(BF16)
        span = pl.ds(strip * LANES, LANES)
        for part in range(2):
            values = spec_buf[part, span, :]
            for position in range(DIR_DEV):
                masked[part, span, position * columns : (position + 1) * columns] = jnp.where(
                    own == jnp.asarray(position, BF16), values, jnp.zeros_like(values)
                )

    def coords_copy(src, owner, to):
        return pltpu.make_async_remote_copy(
            src_ref=coords_out.at[src],
            dst_ref=coords_in.at[owner],
            send_sem=c_send.at[src],
            recv_sem=c_recv.at[owner],
            device_id={"tb": to},
            device_id_type=MESH,
        )

    gain_blocks = group_rows // GB
    pairs = owners // 2

    def models_copy(group, owner, part, to):
        rows = pl.ds(pl.multiple_of(part * GB, GB), GB)
        return pltpu.make_async_remote_copy(
            src_ref=models_out.at[group, rows],
            dst_ref=models_in.at[owner, rows],
            send_sem=m_send.at[part, group],
            recv_sem=m_recv.at[part, owner],
            device_id={"dir": to},
            device_id_type=MESH,
        )

    def send_coords(k, carry):
        to = lax.rem(me_t + k, peers)
        coords_copy(to, me_t, to).start()
        return carry

    def predict_step(step, carry):
        part = lax.rem(step, gain_blocks)
        nearness = step // gain_blocks
        chip = lax.rem(me_d // 2 + 1 + nearness, pairs)
        span = pl.ds(pl.multiple_of(part * GB, GB), GB)
        group_coords = jnp.concatenate(
            [
                coord_rows[
                    pl.ds(
                        pl.multiple_of((2 * chip + side_of) * group_rows + part * GB, GB), GB
                    ),
                    :,
                ]
                for side_of in range(2)
            ],
            axis=0,
        )
        step_rows = 2 * GB
        chunks = comps // CHUNK
        buffers = (turned_a, turned_b)
        pieces = step_rows // SUB

        def spread_turns(chunk):
            return jnp.dot(
                group_coords,
                lm_parts[:, chunk * CHUNK : (chunk + 1) * CHUNK],
                preferred_element_type=F32,
            )

        def contract_chunk(chunk, part):
            return jnp.dot(
                buffers[chunk % 2][part],
                masked[part, chunk * CHUNK : (chunk + 1) * CHUNK, :],
                preferred_element_type=F32,
            )

        turns = spread_turns(0)
        for chunk in range(chunks):
            turned = buffers[chunk % 2]
            following = None
            for sub in range(pieces):
                rows = slice(sub * SUB, (sub + 1) * SUB)
                cos_part, sin_part = turn_cos_sin_short(turns[rows])
                turned[0, rows, :] = cos_part
                turned[1, rows, :] = sin_part
                if chunk > 0 and sub == 0:
                    update = contract_chunk(chunk - 1, 0)
                if chunk > 0 and sub == pieces // 2 - 1:
                    update = update + contract_chunk(chunk - 1, 1)
                    if chunk == 1:
                        acc[...] = update
                    else:
                        acc[...] += update
                if chunk + 1 < chunks and sub == pieces - 2:
                    following = spread_turns(chunk + 1)
            turns = following
        last = contract_chunk(chunks - 1, 0) + contract_chunk(chunks - 1, 1)
        final = (acc[...] + last).astype(BF16)

        @pl.when(step == 0)
        def _():
            pl.semaphore_wait(barrier, owners - 1 + peers - 1)

        for side_of in range(2):
            group = 2 * chip + side_of
            piece = final[side_of * GB : (side_of + 1) * GB]

            @pl.when(group != me_d)
            def _():
                models_out[group, span, :] = piece
                models_copy(group, me_d, part, group).start()

            @pl.when(group == me_d)
            def _():
                models_in[me_d, span, :] = piece

        @pl.when(step == 0)
        def _():
            lax.fori_loop(1, peers, send_coords, 0)

        return carry

    lax.fori_loop(0, pairs * gain_blocks, predict_step, 0)
    coords_in[me_t] = coords_out[me_t]
    index_copy.wait()
    vis_copy.wait()

    ridge = jnp.broadcast_to(ridge_ref[...], (8, columns))
    lane = lax.broadcasted_iota(jnp.int32, (8, columns), 1)
    reach = 2 * (ITERS - 1)

    def over_rows(value):
        total = jnp.sum(jnp.sum(value, axis=0), axis=0, keepdims=True)
        return jnp.broadcast_to(total, (8, columns))

    def moved(value, far):
        rolled = {0: value}
        for shift in range(2, far + 1, 2):
            rolled[shift] = pltpu.roll(value, columns - shift, 1)
            rolled[-shift] = pltpu.roll(value, shift, 1)
        out = {0: value}
        for shift in range(2, far + 1, 2):
            right, left = rolled[shift], rolled[-shift]
            for step in range(shift // 2):
                mirror = shift - 2 - 4 * step
                left = jnp.where(lane // 2 == step, rolled[mirror], left)
                right = jnp.where(lane // 2 == columns // 2 - 1 - step, rolled[-mirror], right)
            out[shift], out[-shift] = right, left
        return out

    def sweep_gain(constant, couple):
        base = moved(constant, reach)
        gain = {shift: base[shift] + 2.0 * couple[shift] for shift in base}
        for sweep in range(1, ITERS):
            far = reach - 2 * sweep
            gain = {
                shift: base[shift] + couple[shift] * (gain[shift - 2] + gain[shift + 2])
                for shift in range(-far, far + 1, 2)
            }
        return gain[0]

    per_gain = GB // BB

    def peel_owner(part, owner, rest):
        models = [
            models_in[
                owner,
                part * GB : (part + 1) * GB,
                position * columns : (position + 1) * columns,
            ]
            .astype(F32)
            .reshape(GB // 8, 8, columns)
            for position in range(DIR_DEV)
        ]
        gains = []
        for position in range(DIR_DEV):
            model = models[position]
            inverse = 1.0 / (over_rows(model * model) + ridge)
            couple = moved(0.5 * ridge * inverse, reach)
            cross_sum = over_rows(rest * model)
            for before in range(position):
                cross_sum = cross_sum - gains[before] * over_rows(models[before] * model)
            gains.append(sweep_gain(cross_sum * inverse, couple))
        for position in range(DIR_DEV):
            rest = rest - gains[position][None] * models[position]
        return rest.astype(BF16).astype(F32)

    def resid_copy(group, part, sem, to):
        span = pl.ds(group * group_blocks + part * per_gain, per_gain)
        return pltpu.make_async_remote_copy(
            src_ref=resid.at[span],
            dst_ref=resid.at[span],
            send_sem=r_send.at[part, sem],
            recv_sem=r_recv.at[part, group],
            device_id={"dir": to},
            device_id_type=MESH,
        )

    for part in range(gain_blocks):
        for k in range(1, owners):
            source = lax.rem(me_d + k, owners)
            models_copy(source, source, part, source).wait()
        rest = (
            vis_buf[part * GB : (part + 1) * GB, :].astype(F32).reshape(GB // 8, 8, columns)
        )
        for owner in range(owners):
            rest = peel_owner(part, owner, rest)
        resid[pl.ds(me_d * group_blocks + part * per_gain, per_gain)] = rest.reshape(
            per_gain, BB, columns
        ).astype(BF16)
        for k in range(1, owners):
            to = lax.rem(me_d + k, owners)
            resid_copy(me_d, part, to, to).start()
    resid[block_count] = jnp.zeros((BB, columns), BF16)
    for part in range(gain_blocks):
        for k in range(1, owners):
            source = lax.rem(me_d + k, owners)
            resid_copy(source, part, source, source).wait_recv()

    def block_in(to, slot):
        block = block_of_ref[0, to * slots + slot]
        return jnp.minimum(jnp.maximum(block, 0), block_count)

    def half_of(which):
        return pl.ds(pl.multiple_of(which * half_rows, half_rows), half_rows)

    def rows_copy(src, owner, to):
        return pltpu.make_async_remote_copy(
            src_ref=rows_out.at[src],
            dst_ref=rows_in.at[owner, half_of(core)],
            send_sem=d_send.at[src],
            recv_sem=d_recv.at[owner],
            device_id={"tb": to},
            device_id_type=MESH,
        )

    def hand_over(owner, which):
        return pltpu.make_async_remote_copy(
            src_ref=rows_in.at[owner, half_of(which)],
            dst_ref=rows_in.at[owner, half_of(which)],
            send_sem=f_send.at[owner],
            recv_sem=f_recv.at[owner],
            device_id={"dir": partner},
            device_id_type=MESH,
        )

    def dispatch(k, carry):
        to = lax.rem(me_t + k, peers)
        for slot in range(half_slots):
            rows_out[to, slot * BB : (slot + 1) * BB, :] = resid[
                block_in(to, core * half_slots + slot)
            ]
        rows_copy(to, me_t, to).start()
        return carry

    lax.fori_loop(1, peers, dispatch, 0)
    for slot in range(slots):
        own_rows[slot * BB : (slot + 1) * BB, :] = resid[block_in(me_t, slot)]
    resid_ref[...] = resid[0:block_count].reshape(sample_rows, columns)

    def wait_coords(k, carry):
        source = lax.rem(me_t + k, peers)
        coords_copy(source, source, source).wait()
        return carry

    lax.fori_loop(1, peers, wait_coords, 0)
    share = grid_ref.shape[1]
    lines = share // GRID
    slots_wide = LANES // BB
    strips_wide = -(-slot_rows // LANES)
    wide = strips_wide * LANES
    x_of = (
        me_d * lines - GRID // 2 + lax.broadcasted_iota(jnp.int32, (lines, wide), 0)
    ).astype(F32) / (2.0 * GRID)
    y_of = (lax.broadcasted_iota(jnp.int32, (GRID, wide), 0) - GRID // 2).astype(F32) / (
        2.0 * GRID
    )
    slot_at = lax.broadcasted_iota(jnp.int32, (side, LANES), 0)
    slot_for = lax.broadcasted_iota(jnp.int32, (side, LANES), 1) // BB

    def make_table(source, carry):
        given = coords_in[source].astype(F32)

        def flat(rows):
            return jnp.concatenate(
                [
                    jnp.sum(
                        jnp.where(slot_at == slot_for + strip * slots_wide, rows, 0.0),
                        axis=0,
                        keepdims=True,
                    )
                    for strip in range(strips_wide)
                ],
                axis=1,
            )

        cos_x, sin_x = turn_cos_sin(x_of * flat(given[0:side]))
        cos_y, sin_y = turn_cos_sin(y_of * flat(given[side:packed]))
        for line in range(lines):
            cos_l, sin_l = cos_x[line : line + 1], sin_x[line : line + 1]
            rows = slice(line * GRID, (line + 1) * GRID)
            lower = slice(share + line * GRID, share + (line + 1) * GRID)
            cos_part = (cos_l * cos_y - sin_l * sin_y).astype(BF16)
            sin_part = (sin_l * cos_y + cos_l * sin_y).astype(BF16)
            tables[source, rows, :] = cos_part[:, 0:slot_rows]
            tables[source, lower, :] = sin_part[:, 0:slot_rows]
        return carry

    lax.fori_loop(0, peers, make_table, 0)

    grid_sum = jnp.dot(tables[me_t], own_rows[...], preferred_element_type=F32)

    def source_at(k):
        return lax.rem(me_t + peers - k, peers)

    def arrive(k):
        source = source_at(k)
        rows_copy(source, source, source).wait_recv()
        hand_over(source, core).start()

    def add_source(k, total):
        @pl.when(k + 1 < peers)
        def _():
            arrive(k + 1)

        source = source_at(k)
        hand_over(source, 1 - core).wait_recv()
        return total + jnp.dot(tables[source], rows_in[source], preferred_element_type=F32)

    arrive(1)
    grid_sum = lax.fori_loop(1, peers, add_source, grid_sum)
    grid_ref[...] = (grid_sum * float(ROWS_DEV) ** (-0.5)).reshape(2, share, columns)

    for part in range(gain_blocks):
        for k in range(1, owners):
            to = lax.rem(me_d + k, owners)
            resid_copy(me_d, part, to, to).wait_send()

    def drain(k, carry):
        to = lax.rem(me_t + k, peers)
        rows_copy(to, me_t, to).wait_send()
        hand_over(to, core).wait_send()
        return carry

    lax.fori_loop(1, peers, drain, 0)


def finish(resid_ref, grid_ref, resid_out, grid_out, sem):
    copies = (
        pltpu.make_async_copy(resid_ref, resid_out, sem.at[0]),
        pltpu.make_async_copy(grid_ref, grid_out, sem.at[1]),
    )
    for copy in copies:
        copy.start()
    for copy in copies:
        copy.wait()


def local(
    owners,
    peers,
    visibilities,
    uv_coords,
    comp_lm,
    spectra,
    ridge_weight,
    assignment,
    peel_order,
    block_tile,
):
    sample_rows, columns = visibilities.shape
    comps = comp_lm.shape[1]
    block_count = sample_rows // BB
    slots = max(2, 2 * block_count // peers)
    share = PIX // owners

    slot_lanes = -(-peers * slots // LANES) * LANES
    packed = 16 * -(-slots // 8)
    group_rows = sample_rows // owners
    half_rows = slots // 2 * BB
    vmem = pl.BlockSpec(memory_space=pltpu.VMEM)
    smem = pl.BlockSpec(memory_space=pltpu.SMEM)
    anywhere = pl.BlockSpec(memory_space=pl.ANY)
    dma = pltpu.SemaphoreType.DMA
    residual, subgrid = pl.pallas_call(
        functools.partial(kernel, owners, peers, slots),
        out_shape=(
            pltpu.VMEM((sample_rows, columns), BF16),
            pltpu.VMEM((2, share, columns), F32),
        ),
        in_specs=[vmem] * 5 + [smem] + [anywhere] * 2,
        out_specs=(vmem, vmem),
        scratch_shapes=[
            pltpu.VMEM((group_rows, columns), BF16),
            pltpu.VMEM((2, comps, columns), BF16),
            pltpu.VMEM((2, comps, DIR_DEV * columns), BF16),
            pltpu.VMEM((8, comps), BF16),
            pltpu.VMEM((sample_rows, 8), BF16),
            pltpu.VMEM((1, slot_lanes), jnp.int32),
            pltpu.SMEM((1, slot_lanes), jnp.int32),
            pltpu.VMEM((peers, packed, LANES), BF16),
            pltpu.VMEM((2, 2 * GB, CHUNK), BF16),
            pltpu.VMEM((2, 2 * GB, CHUNK), BF16),
            pltpu.VMEM((2 * GB, DIR_DEV * columns), F32),
            pltpu.VMEM((owners, group_rows, DIR_DEV * columns), BF16),
            pltpu.VMEM((owners, group_rows, DIR_DEV * columns), BF16),
            pltpu.VMEM((block_count + 1, BB, columns), BF16),
            pltpu.VMEM((slots * BB, columns), BF16),
            pltpu.VMEM((peers, half_rows, columns), BF16),
            pltpu.VMEM((peers, slots * BB, columns), BF16),
            pltpu.VMEM((peers, packed, LANES), BF16),
            pltpu.VMEM((peers, 2 * share, slots * BB), BF16),
            dma((group_rows // GB, owners)),
            dma((group_rows // GB, owners)),
            dma((group_rows // GB, owners)),
            dma((group_rows // GB, owners)),
            dma((peers,)),
            dma((peers,)),
            dma((peers,)),
            dma((peers,)),
            dma((peers,)),
            dma((peers,)),
            dma((3,)),
        ],
        compiler_params=pltpu.CompilerParams(
            collective_id=0, has_side_effects=True, vmem_limit_bytes=60 * 1024 * 1024
        ),
    )(
        uv_coords,
        comp_lm,
        ridge_weight[None, :],
        assignment.reshape(comps // LANES, LANES),
        block_tile.reshape(1, block_count),
        peel_order,
        visibilities,
        spectra,
    )
    residual, subgrid = pl.pallas_call(
        finish,
        out_shape=(
            jax.ShapeDtypeStruct(residual.shape, residual.dtype),
            jax.ShapeDtypeStruct(subgrid.shape, subgrid.dtype),
        ),
        in_specs=[vmem] * 2,
        out_specs=(anywhere, anywhere),
        scratch_shapes=[dma((2,))],
    )(
        pltpu.with_memory_space_constraint(residual, pltpu.VMEM),
        pltpu.with_memory_space_constraint(subgrid, pltpu.VMEM),
    )
    return residual, subgrid[None]


def solution(mesh):
    return jax.shard_map(
        functools.partial(local, mesh.shape["dir"], mesh.shape["tb"]),
        mesh=mesh,
        in_specs=(
            P("tb", None),
            P(None, "tb"),
            P(None, "dir"),
            P(None, "dir", None),
            P(),
            P("dir"),
            P("dir"),
            P("tb", None),
        ),
        out_specs=(P("tb", None), P("tb", None, "dir", None)),
        check_vma=False,
    )
```

```python
import functools
import math

import jax
import jax.numpy as jnp
from jax import lax
from jax.experimental import pallas as pl
from jax.experimental.pallas import tpu as pltpu
from jax.sharding import PartitionSpec as P

NCOMP = 1024
GRID = 32
DIR_DEV = 3
ITERS = 4
BB = 32
GB = 128
ROWS_DEV = 1024
PIX = 1024

MESH = pl.DeviceIdType.MESH
F32 = jnp.float32
BF16 = jnp.bfloat16
LANES = 128
CHUNK = 256
SUB = 32

SIN_FIT = (4.4428795675460835, -7.307816684491791, 3.5977741780872416, -0.7911993921613704)
COS_FIT = (1.414204014809076, -6.977637323456295, 5.715187874756718, -1.728213892223522)


BENT_SIN = (6.28125, -41.25, 76.5)
BENT_COS = (1.0, -19.75, 65.0, -79.5)


def horner(square, fit):
    total = jnp.asarray(fit[-1], square.dtype)
    for coefficient in fit[-2::-1]:
        total = total * square + jnp.asarray(coefficient, square.dtype)
    return total


def turn_cos_sin(turns):
    part = turns - jnp.round(turns)
    square = part * part
    half_sin = part * horner(square, SIN_FIT)
    half_cos = horner(square, COS_FIT)
    return 1.0 - half_sin * half_sin, half_sin * half_cos


def turn_cos_sin_short(turns):
    part = turns - jnp.round(turns)
    bent = (0.25 - jnp.abs(part)).astype(BF16)
    square = bent * bent
    upright = horner(square, BENT_COS)
    flipped = jnp.where(part.astype(BF16) < 0, -upright, upright)
    return bent * horner(square, BENT_SIN), flipped


def kernel(
    owners,
    peers,
    slots,
    lm_hbm,
    entry_hbm,
    peel_hbm,
    uv_hbm,
    spec_hbm,
    vis_hbm,
    ridge_hbm,
    tile_hbm,
    resid_ref,
    grid_ref,
    lm_ref,
    entry_ref,
    peel_ref,
    uv_ref,
    spec_buf,
    vis_buf,
    ridge_ref,
    tile_ref,
    masked,
    lm_parts,
    coord_rows,
    block_row,
    block_of_ref,
    coords_out,
    turned_a,
    turned_b,
    acc,
    models_out,
    models_in,
    resid,
    own_rows,
    rows_out,
    rows_in,
    coords_in,
    tables,
    m_send,
    m_recv,
    r_send,
    r_recv,
    d_send,
    d_recv,
    f_send,
    f_recv,
    c_send,
    c_recv,
    local_sem,
):
    me_d = lax.axis_index("dir")
    me_t = lax.axis_index("tb")
    core = me_d % 2
    partner = me_d + 1 - 2 * core
    group_rows, columns = vis_buf.shape
    sample_rows = group_rows * owners
    comps = lm_ref.shape[1]
    block_count = sample_rows // BB
    group_blocks = block_count // owners
    slot_rows = slots * BB
    half_slots = slots // 2
    half_rows = half_slots * BB
    first = me_d * group_rows

    own_part = vis_hbm.at[pl.ds(pl.multiple_of(first, group_rows), group_rows)]
    fetches = [
        pltpu.make_async_copy(source, target, local_sem.at[number])
        for number, (source, target) in enumerate(
            (
                (lm_hbm, lm_ref),
                (entry_hbm, entry_ref),
                (peel_hbm, peel_ref),
                (uv_hbm, uv_ref),
                (spec_hbm, spec_buf),
                (own_part, vis_buf),
                (ridge_hbm, ridge_ref),
                (tile_hbm, tile_ref),
            )
        )
    ]
    for fetch in fetches:
        fetch.start()

    barrier = pltpu.get_barrier_semaphore()
    for k in range(1, owners):
        pl.semaphore_signal(
            barrier, inc=1, device_id={"dir": lax.rem(me_d + k, owners)}, device_id_type=MESH
        )

    def greet(k, carry):
        pl.semaphore_signal(
            barrier, inc=1, device_id={"tb": lax.rem(me_t + k, peers)}, device_id_type=MESH
        )
        return carry

    lax.fori_loop(1, peers, greet, 0)

    for fetch in fetches[0:4]:
        fetch.wait()

    u_row = uv_ref[0:1, :].astype(F32)
    v_row = uv_ref[1:2, :].astype(F32)
    stacked = jnp.concatenate(
        [u_row] * 3 + [v_row] * 3 + [jnp.zeros((2, sample_rows), F32)], axis=0
    )
    coord_rows[...] = stacked.T.astype(BF16)

    parts = []
    for which in range(2):
        left = lm_ref[which : which + 1, :]
        for part in range(3):
            rounded = left.astype(BF16).astype(F32)
            parts.append(rounded)
            left = left - rounded
    parts.append(jnp.zeros((2, comps), F32))
    lm_parts[...] = jnp.concatenate(parts, axis=0).astype(BF16)

    strips = comps // LANES
    padded = -(-strips // 16) * 16
    named = jnp.concatenate([entry_ref[r : r + 1, :] for r in range(strips)], axis=1)
    places = []
    for direction in range(DIR_DEV):
        value = jnp.int32(0)
        for position in range(DIR_DEV):
            value = value + jnp.where(peel_ref[position] == direction, position, 0)
        places.append(jnp.full((1, comps // DIR_DEV), value, jnp.int32))
    place = jnp.concatenate(places, axis=1).astype(F32)
    low = lax.broadcasted_iota(jnp.int32, (LANES, comps), 0)
    high = lax.broadcasted_iota(jnp.int32, (padded, comps), 0)
    at_low = jnp.where(low == named % LANES, 1.0, 0.0).astype(BF16)
    at_high = jnp.where(high == named // LANES, place, 0.0).astype(BF16)
    positions = lax.dot_general(
        at_low, at_high, (((1,), (1,)), ((), ())), preferred_element_type=F32
    )
    fetches[4].wait()
    for strip in range(strips):
        own = jnp.broadcast_to(positions[:, strip : strip + 1], (LANES, columns)).astype(BF16)
        span = pl.ds(strip * LANES, LANES)
        chunk, inside = strip * LANES // CHUNK, strip * LANES % CHUNK
        for part in range(2):
            values = spec_buf[part, span, :]
            target_span = pl.ds((2 * chunk + part) * CHUNK + inside, LANES)
            for position in range(DIR_DEV):
                masked[target_span, position * columns : (position + 1) * columns] = jnp.where(
                    own == jnp.asarray(position, BF16), values, jnp.zeros_like(values)
                )

    def coords_copy(src, owner, to):
        return pltpu.make_async_remote_copy(
            src_ref=coords_out.at[src],
            dst_ref=coords_in.at[owner],
            send_sem=c_send.at[src],
            recv_sem=c_recv.at[owner],
            device_id={"tb": to},
            device_id_type=MESH,
        )

    gain_blocks = group_rows // GB
    pairs = owners // 2

    def models_copy(group, owner, part, to):
        rows = pl.ds(pl.multiple_of(part * GB, GB), GB)
        return pltpu.make_async_remote_copy(
            src_ref=models_out.at[group, rows],
            dst_ref=models_in.at[owner, rows],
            send_sem=m_send.at[part, group],
            recv_sem=m_recv.at[part, owner],
            device_id={"dir": to},
            device_id_type=MESH,
        )

    def send_coords(k, carry):
        to = lax.rem(me_t + k, peers)
        coords_copy(to, me_t, to).start()
        return carry

    def predict_step(step, carry):
        part = lax.rem(step, gain_blocks)
        nearness = step // gain_blocks
        chip = lax.rem(me_d // 2 + 1 + nearness, pairs)
        span = pl.ds(pl.multiple_of(part * GB, GB), GB)
        group_coords = jnp.concatenate(
            [
                coord_rows[
                    pl.ds(
                        pl.multiple_of((2 * chip + side_of) * group_rows + part * GB, GB), GB
                    ),
                    :,
                ]
                for side_of in range(2)
            ],
            axis=0,
        )
        step_rows = 2 * GB
        chunks = comps // CHUNK
        buffers = (turned_a, turned_b)
        pieces = step_rows // SUB

        def spread_turns(chunk):
            return jnp.dot(
                group_coords,
                lm_parts[:, chunk * CHUNK : (chunk + 1) * CHUNK],
                preferred_element_type=F32,
            )

        def contract_chunk(chunk):
            return jnp.dot(
                buffers[chunk % 2][...],
                masked[2 * chunk * CHUNK : 2 * (chunk + 1) * CHUNK, :],
                preferred_element_type=F32,
            )

        turns = spread_turns(0)
        for chunk in range(chunks):
            turned = buffers[chunk % 2]
            following = None
            for sub in range(pieces):
                rows = slice(sub * SUB, (sub + 1) * SUB)
                cos_part, sin_part = turn_cos_sin_short(turns[rows])
                turned[rows, 0:CHUNK] = cos_part
                turned[rows, CHUNK : 2 * CHUNK] = sin_part
                if chunk > 0 and sub == 0:
                    update = contract_chunk(chunk - 1)
                    if chunk == 1:
                        acc[...] = update
                    else:
                        acc[...] += update
                if chunk + 1 < chunks and sub == pieces - 2:
                    following = spread_turns(chunk + 1)
            turns = following
        last = contract_chunk(chunks - 1)
        final = (acc[...] + last).astype(BF16)

        @pl.when(step == 0)
        def _():
            pl.semaphore_wait(barrier, owners - 1 + peers - 1)

        for side_of in range(2):
            group = 2 * chip + side_of
            piece = final[side_of * GB : (side_of + 1) * GB]

            @pl.when(group != me_d)
            def _():
                models_out[group, span, :] = piece
                models_copy(group, me_d, part, group).start()

            @pl.when(group == me_d)
            def _():
                models_in[me_d, span, :] = piece

        return carry

    lax.fori_loop(0, pairs * gain_blocks, predict_step, 0)
    for fetch in fetches[5:]:
        fetch.wait()


    ridge = jnp.broadcast_to(ridge_ref[...], (8, columns))
    lane = lax.broadcasted_iota(jnp.int32, (8, columns), 1)
    reach = 2 * (ITERS - 1)

    def over_rows(value):
        total = jnp.sum(jnp.sum(value, axis=0), axis=0, keepdims=True)
        return jnp.broadcast_to(total, (8, columns))

    def moved(value, far):
        rolled = {0: value}
        for shift in range(2, far + 1, 2):
            rolled[shift] = pltpu.roll(value, columns - shift, 1)
            rolled[-shift] = pltpu.roll(value, shift, 1)
        out = {0: value}
        for shift in range(2, far + 1, 2):
            right, left = rolled[shift], rolled[-shift]
            for step in range(shift // 2):
                mirror = shift - 2 - 4 * step
                left = jnp.where(lane // 2 == step, rolled[mirror], left)
                right = jnp.where(lane // 2 == columns // 2 - 1 - step, rolled[-mirror], right)
            out[shift], out[-shift] = right, left
        return out

    def sweep_gain(constant, couple):
        base = moved(constant, reach)
        gain = {shift: base[shift] + 2.0 * couple[shift] for shift in base}
        for sweep in range(1, ITERS):
            far = reach - 2 * sweep
            gain = {
                shift: base[shift] + couple[shift] * (gain[shift - 2] + gain[shift + 2])
                for shift in range(-far, far + 1, 2)
            }
        return gain[0]

    per_gain = GB // BB

    def peel_owner(part, owner, rest):
        models = [
            models_in[
                owner,
                part * GB : (part + 1) * GB,
                position * columns : (position + 1) * columns,
            ]
            .astype(F32)
            .reshape(GB // 8, 8, columns)
            for position in range(DIR_DEV)
        ]
        gains = []
        for position in range(DIR_DEV):
            model = models[position]
            inverse = 1.0 / (over_rows(model * model) + ridge)
            couple = moved(0.5 * ridge * inverse, reach)
            cross_sum = over_rows(rest * model)
            for before in range(position):
                cross_sum = cross_sum - gains[before] * over_rows(models[before] * model)
            gains.append(sweep_gain(cross_sum * inverse, couple))
        for position in range(DIR_DEV):
            rest = rest - gains[position][None] * models[position]
        return rest.astype(BF16).astype(F32)

    def resid_copy(group, part, sem, to):
        span = pl.ds(group * group_blocks + part * per_gain, per_gain)
        return pltpu.make_async_remote_copy(
            src_ref=resid.at[span],
            dst_ref=resid.at[span],
            send_sem=r_send.at[part, sem],
            recv_sem=r_recv.at[part, group],
            device_id={"dir": to},
            device_id_type=MESH,
        )

    for part in range(gain_blocks):
        for k in range(1, owners):
            source = lax.rem(me_d + k, owners)
            models_copy(source, source, part, source).wait()
        rest = (
            vis_buf[part * GB : (part + 1) * GB, :].astype(F32).reshape(GB // 8, 8, columns)
        )
        for owner in range(owners):
            rest = peel_owner(part, owner, rest)
        resid[pl.ds(me_d * group_blocks + part * per_gain, per_gain)] = rest.reshape(
            per_gain, BB, columns
        ).astype(BF16)
        for k in range(1, owners):
            to = lax.rem(me_d + k, owners)
            resid_copy(me_d, part, to, to).start()
    resid[block_count] = jnp.zeros((BB, columns), BF16)

    slot_lanes = block_row.shape[1]
    tiles = jnp.broadcast_to(tile_ref[...], (slot_lanes, block_count))
    named_tile = jnp.where(
        lax.broadcasted_iota(jnp.int32, (slot_lanes, block_count), 0) == tiles, 1.0, 0.0
    )
    earlier = jnp.where(
        lax.broadcasted_iota(jnp.int32, (block_count, block_count), 0)
        < lax.broadcasted_iota(jnp.int32, (block_count, block_count), 1),
        1.0,
        0.0,
    )
    ranks = jnp.dot(named_tile.astype(BF16), earlier.astype(BF16), preferred_element_type=F32)
    slot = jnp.sum(ranks * named_tile, axis=0, keepdims=True).astype(jnp.int32)
    target = jnp.broadcast_to(tile_ref[...] * slots + slot, (slot_lanes, block_count))
    lane = lax.broadcasted_iota(jnp.int32, (slot_lanes, block_count), 0)
    taken = jnp.where(lane == target, 1.0, 0.0).astype(BF16)
    block_id = lax.broadcasted_iota(jnp.int32, (8, block_count), 1) - block_count
    picked = lax.dot_general(
        block_id.astype(F32).astype(BF16),
        taken,
        (((1,), (1,)), ((), ())),
        preferred_element_type=F32,
    )
    block_row[...] = picked[0:1, :].astype(jnp.int32) + block_count
    index_copy = pltpu.make_async_copy(block_row, block_of_ref, local_sem.at[len(fetches)])
    index_copy.start()

    in_block = (
        lax.broadcasted_iota(jnp.int32, (block_count, sample_rows), 1) // BB
        == lax.broadcasted_iota(jnp.int32, (block_count, sample_rows), 0)
    )
    at_lane = jnp.where(
        lax.broadcasted_iota(jnp.int32, (sample_rows, LANES), 0) % BB
        == lax.broadcasted_iota(jnp.int32, (sample_rows, LANES), 1) % BB,
        1.0,
        0.0,
    ).astype(BF16)
    packed, side = coords_out.shape[1], coords_out.shape[1] // 2
    spot = lax.broadcasted_iota(jnp.int32, (peers * packed, block_count), 0)
    place_of = tile_ref[...] * packed + slot
    sent = jnp.zeros((peers * packed, LANES), F32)
    for which, row in enumerate((u_row, v_row)):
        spread = jnp.where(in_block, jnp.broadcast_to(row, in_block.shape), 0.0).astype(BF16)
        by_block = jnp.dot(spread, at_lane, preferred_element_type=F32).astype(BF16)
        chosen = jnp.where(spot == place_of + which * side, 1.0, 0.0).astype(BF16)
        sent = sent + jnp.dot(chosen, by_block, preferred_element_type=F32)
    coords_out[...] = sent.astype(BF16).reshape(peers, packed, LANES)

    lax.fori_loop(1, peers, send_coords, 0)
    coords_in[me_t] = coords_out[me_t]
    index_copy.wait()

    for part in range(gain_blocks):
        for k in range(1, owners):
            source = lax.rem(me_d + k, owners)
            resid_copy(source, part, source, source).wait_recv()

    def block_in(to, slot):
        block = block_of_ref[0, to * slots + slot]
        return jnp.minimum(jnp.maximum(block, 0), block_count)

    def half_of(which):
        return pl.ds(pl.multiple_of(which * half_rows, half_rows), half_rows)

    def rows_copy(src, owner, to):
        return pltpu.make_async_remote_copy(
            src_ref=rows_out.at[src],
            dst_ref=rows_in.at[owner, half_of(core)],
            send_sem=d_send.at[src],
            recv_sem=d_recv.at[owner],
            device_id={"tb": to},
            device_id_type=MESH,
        )

    def hand_over(owner, which):
        return pltpu.make_async_remote_copy(
            src_ref=rows_in.at[owner, half_of(which)],
            dst_ref=rows_in.at[owner, half_of(which)],
            send_sem=f_send.at[owner],
            recv_sem=f_recv.at[owner],
            device_id={"dir": partner},
            device_id_type=MESH,
        )

    def paired(k):
        other, bit = 0, 1
        while bit < peers:
            other = other + bit * ((me_t // bit + k // bit) % 2)
            bit = 2 * bit
        return other

    def dispatch(k, carry):
        to = lax.rem(me_t + k, peers)
        for slot in range(half_slots):
            rows_out[to, slot * BB : (slot + 1) * BB, :] = resid[
                block_in(to, core * half_slots + slot)
            ]
        rows_copy(to, me_t, to).start()
        return carry

    lax.fori_loop(1, peers, dispatch, 0)
    for slot in range(slots):
        own_rows[slot * BB : (slot + 1) * BB, :] = resid[block_in(me_t, slot)]
    resid_ref[...] = resid[0:block_count].reshape(sample_rows, columns)

    def wait_coords(k, carry):
        source = lax.rem(me_t + k, peers)
        coords_copy(source, source, source).wait()
        return carry

    lax.fori_loop(1, peers, wait_coords, 0)
    share = grid_ref.shape[1]
    lines = share // GRID
    slots_wide = LANES // BB
    strips_wide = -(-slot_rows // LANES)
    wide = strips_wide * LANES
    x_of = (
        me_d * lines - GRID // 2 + lax.broadcasted_iota(jnp.int32, (lines, wide), 0)
    ).astype(F32) / (2.0 * GRID)
    y_of = (lax.broadcasted_iota(jnp.int32, (GRID, wide), 0) - GRID // 2).astype(F32) / (
        2.0 * GRID
    )
    slot_at = lax.broadcasted_iota(jnp.int32, (side, LANES), 0)
    slot_for = lax.broadcasted_iota(jnp.int32, (side, LANES), 1) // BB

    def make_table(source, carry):
        given = coords_in[source].astype(F32)

        def flat(rows):
            return jnp.concatenate(
                [
                    jnp.sum(
                        jnp.where(slot_at == slot_for + strip * slots_wide, rows, 0.0),
                        axis=0,
                        keepdims=True,
                    )
                    for strip in range(strips_wide)
                ],
                axis=1,
            )

        cos_x, sin_x = turn_cos_sin(x_of * flat(given[0:side]))
        cos_y, sin_y = turn_cos_sin(y_of * flat(given[side:packed]))
        for line in range(lines):
            cos_l, sin_l = cos_x[line : line + 1], sin_x[line : line + 1]
            rows = slice(line * GRID, (line + 1) * GRID)
            lower = slice(share + line * GRID, share + (line + 1) * GRID)
            cos_part = (cos_l * cos_y - sin_l * sin_y).astype(BF16)
            sin_part = (sin_l * cos_y + cos_l * sin_y).astype(BF16)
            tables[source, rows, :] = cos_part[:, 0:slot_rows]
            tables[source, lower, :] = sin_part[:, 0:slot_rows]
        return carry

    lax.fori_loop(0, peers, make_table, 0)

    grid_sum = jnp.dot(tables[me_t], own_rows[...], preferred_element_type=F32)

    def source_at(k):
        return paired(k)

    def arrive(k):
        source = source_at(k)
        rows_copy(source, source, source).wait_recv()
        hand_over(source, core).start()

    def add_source(k, total):
        @pl.when(k + 3 < peers)
        def _():
            arrive(k + 3)

        source = source_at(k)
        hand_over(source, 1 - core).wait_recv()
        return total + jnp.dot(tables[source], rows_in[source], preferred_element_type=F32)

    for ahead in range(1, min(3, peers - 1) + 1):
        arrive(ahead)
    grid_sum = lax.fori_loop(1, peers, add_source, grid_sum)
    grid_ref[...] = (grid_sum * float(ROWS_DEV) ** (-0.5)).reshape(2, share, columns)

    for part in range(gain_blocks):
        for k in range(1, owners):
            to = lax.rem(me_d + k, owners)
            resid_copy(me_d, part, to, to).wait_send()

    def drain(k, carry):
        to = lax.rem(me_t + k, peers)
        rows_copy(to, me_t, to).wait_send()
        hand_over(to, core).wait_send()
        return carry

    lax.fori_loop(1, peers, drain, 0)


def finish(resid_ref, grid_ref, resid_out, grid_out, sem):
    copies = (
        pltpu.make_async_copy(resid_ref, resid_out, sem.at[0]),
        pltpu.make_async_copy(grid_ref, grid_out, sem.at[1]),
    )
    for copy in copies:
        copy.start()
    for copy in copies:
        copy.wait()


def local(
    owners,
    peers,
    visibilities,
    uv_coords,
    comp_lm,
    spectra,
    ridge_weight,
    assignment,
    peel_order,
    block_tile,
):
    sample_rows, columns = visibilities.shape
    comps = comp_lm.shape[1]
    block_count = sample_rows // BB
    slots = max(2, 2 * block_count // peers)
    share = PIX // owners

    slot_lanes = -(-peers * slots // LANES) * LANES
    packed = 16 * -(-slots // 8)
    group_rows = sample_rows // owners
    half_rows = slots // 2 * BB
    vmem = pl.BlockSpec(memory_space=pltpu.VMEM)
    anywhere = pl.BlockSpec(memory_space=pl.ANY)
    dma = pltpu.SemaphoreType.DMA
    residual, subgrid = pl.pallas_call(
        functools.partial(kernel, owners, peers, slots),
        out_shape=(
            pltpu.VMEM((sample_rows, columns), BF16),
            pltpu.VMEM((2, share, columns), F32),
        ),
        in_specs=[anywhere] * 8,
        out_specs=(vmem, vmem),
        scratch_shapes=[
            pltpu.VMEM((2, comps), F32),
            pltpu.VMEM((comps // LANES, LANES), jnp.int32),
            pltpu.SMEM((DIR_DEV,), jnp.int32),
            pltpu.VMEM((2, sample_rows), BF16),
            pltpu.VMEM((2, comps, columns), BF16),
            pltpu.VMEM((group_rows, columns), BF16),
            pltpu.VMEM((1, columns), F32),
            pltpu.VMEM((1, block_count), jnp.int32),
            pltpu.VMEM((2 * comps, DIR_DEV * columns), BF16),
            pltpu.VMEM((8, comps), BF16),
            pltpu.VMEM((sample_rows, 8), BF16),
            pltpu.VMEM((1, slot_lanes), jnp.int32),
            pltpu.SMEM((1, slot_lanes), jnp.int32),
            pltpu.VMEM((peers, packed, LANES), BF16),
            pltpu.VMEM((2 * GB, 2 * CHUNK), BF16),
            pltpu.VMEM((2 * GB, 2 * CHUNK), BF16),
            pltpu.VMEM((2 * GB, DIR_DEV * columns), F32),
            pltpu.VMEM((owners, group_rows, DIR_DEV * columns), BF16),
            pltpu.VMEM((owners, group_rows, DIR_DEV * columns), BF16),
            pltpu.VMEM((block_count + 1, BB, columns), BF16),
            pltpu.VMEM((slots * BB, columns), BF16),
            pltpu.VMEM((peers, half_rows, columns), BF16),
            pltpu.VMEM((peers, slots * BB, columns), BF16),
            pltpu.VMEM((peers, packed, LANES), BF16),
            pltpu.VMEM((peers, 2 * share, slots * BB), BF16),
            dma((group_rows // GB, owners)),
            dma((group_rows // GB, owners)),
            dma((group_rows // GB, owners)),
            dma((group_rows // GB, owners)),
            dma((peers,)),
            dma((peers,)),
            dma((peers,)),
            dma((peers,)),
            dma((peers,)),
            dma((peers,)),
            dma((9,)),
        ],
        compiler_params=pltpu.CompilerParams(
            collective_id=0, has_side_effects=True, vmem_limit_bytes=60 * 1024 * 1024
        ),
    )(
        comp_lm,
        assignment.reshape(comps // LANES, LANES),
        peel_order,
        uv_coords,
        spectra,
        visibilities,
        ridge_weight[None, :],
        block_tile.reshape(1, block_count),
    )
    residual, subgrid = pl.pallas_call(
        finish,
        out_shape=(
            jax.ShapeDtypeStruct(residual.shape, residual.dtype),
            jax.ShapeDtypeStruct(subgrid.shape, subgrid.dtype),
        ),
        in_specs=[vmem] * 2,
        out_specs=(anywhere, anywhere),
        scratch_shapes=[dma((2,))],
    )(
        pltpu.with_memory_space_constraint(residual, pltpu.VMEM),
        pltpu.with_memory_space_constraint(subgrid, pltpu.VMEM),
    )
    return residual, subgrid[None]


def solution(mesh):
    return jax.shard_map(
        functools.partial(local, mesh.shape["dir"], mesh.shape["tb"]),
        mesh=mesh,
        in_specs=(
            P("tb", None),
            P(None, "tb"),
            P(None, "dir"),
            P(None, "dir", None),
            P(),
            P("dir"),
            P("dir"),
            P("tb", None),
        ),
        out_specs=(P("tb", None), P("tb", None, "dir", None)),
        check_vma=False,
    )
```

```python
import functools
import math

import jax
import jax.numpy as jnp
from jax import lax
from jax.experimental import pallas as pl
from jax.experimental.pallas import tpu as pltpu
from jax.sharding import PartitionSpec as P

NCOMP = 1024
GRID = 32
DIR_DEV = 3
ITERS = 4
BB = 32
GB = 128
ROWS_DEV = 1024
PIX = 1024

MESH = pl.DeviceIdType.MESH
F32 = jnp.float32
BF16 = jnp.bfloat16
LANES = 128
CHUNK = 256
SUB = 32

SIN_FIT = (4.4428795675460835, -7.307816684491791, 3.5977741780872416, -0.7911993921613704)
COS_FIT = (1.414204014809076, -6.977637323456295, 5.715187874756718, -1.728213892223522)


BENT_SIN = (6.28125, -41.25, 76.5)
BENT_COS = (1.0, -19.75, 65.0, -79.5)


def horner(square, fit):
    total = jnp.asarray(fit[-1], square.dtype)
    for coefficient in fit[-2::-1]:
        total = total * square + jnp.asarray(coefficient, square.dtype)
    return total


def turn_cos_sin(turns):
    part = turns - jnp.round(turns)
    square = part * part
    half_sin = part * horner(square, SIN_FIT)
    half_cos = horner(square, COS_FIT)
    return 1.0 - half_sin * half_sin, half_sin * half_cos


def turn_cos_sin_short(turns):
    part = turns - jnp.round(turns)
    bent = (0.25 - jnp.abs(part)).astype(BF16)
    square = bent * bent
    upright = horner(square, BENT_COS)
    flipped = jnp.where(part.astype(BF16) < 0, -upright, upright)
    return bent * horner(square, BENT_SIN), flipped


def kernel(
    owners,
    peers,
    slots,
    lm_hbm,
    entry_hbm,
    peel_hbm,
    uv_hbm,
    spec_hbm,
    vis_hbm,
    ridge_hbm,
    tile_hbm,
    resid_ref,
    grid_ref,
    lm_ref,
    entry_ref,
    peel_ref,
    uv_ref,
    spec_buf,
    vis_buf,
    ridge_ref,
    tile_ref,
    masked,
    lm_parts,
    coord_rows,
    block_row,
    block_of_ref,
    coords_out,
    turned_a,
    turned_b,
    acc,
    models_out,
    models_in,
    resid,
    own_rows,
    rows_out,
    rows_in,
    coords_in,
    tables,
    m_send,
    m_recv,
    r_send,
    r_recv,
    d_send,
    d_recv,
    f_send,
    f_recv,
    c_send,
    c_recv,
    local_sem,
):
    me_d = lax.axis_index("dir")
    me_t = lax.axis_index("tb")
    core = me_d % 2
    partner = me_d + 1 - 2 * core
    group_rows, columns = vis_buf.shape
    sample_rows = group_rows * owners
    comps = lm_ref.shape[1]
    block_count = sample_rows // BB
    group_blocks = block_count // owners
    slot_rows = slots * BB
    half_slots = slots // 2
    half_rows = half_slots * BB
    first = me_d * group_rows

    own_part = vis_hbm.at[pl.ds(pl.multiple_of(first, group_rows), group_rows)]
    fetches = [
        pltpu.make_async_copy(source, target, local_sem.at[number])
        for number, (source, target) in enumerate(
            (
                (lm_hbm, lm_ref),
                (entry_hbm, entry_ref),
                (peel_hbm, peel_ref),
                (uv_hbm, uv_ref),
                (spec_hbm.at[0], spec_buf.at[:, 0:columns]),
                (spec_hbm.at[1], spec_buf.at[:, columns : 2 * columns]),
                (own_part, vis_buf),
                (ridge_hbm, ridge_ref),
                (tile_hbm, tile_ref),
            )
        )
    ]
    for fetch in fetches:
        fetch.start()

    barrier = pltpu.get_barrier_semaphore()
    for k in range(1, owners):
        pl.semaphore_signal(
            barrier, inc=1, device_id={"dir": lax.rem(me_d + k, owners)}, device_id_type=MESH
        )

    def greet(k, carry):
        pl.semaphore_signal(
            barrier, inc=1, device_id={"tb": lax.rem(me_t + k, peers)}, device_id_type=MESH
        )
        return carry

    lax.fori_loop(1, peers, greet, 0)

    for fetch in fetches[0:4]:
        fetch.wait()

    u_row = uv_ref[0:1, :].astype(F32)
    v_row = uv_ref[1:2, :].astype(F32)
    stacked = jnp.concatenate(
        [u_row] * 3 + [v_row] * 3 + [jnp.zeros((2, sample_rows), F32)], axis=0
    )
    coord_rows[...] = stacked.T.astype(BF16)

    parts = []
    for which in range(2):
        left = lm_ref[which : which + 1, :]
        for part in range(3):
            rounded = left.astype(BF16).astype(F32)
            parts.append(rounded)
            left = left - rounded
    parts.append(jnp.zeros((2, comps), F32))
    lm_parts[...] = jnp.concatenate(parts, axis=0).astype(BF16)

    strips = comps // LANES
    padded = -(-strips // 16) * 16
    named = jnp.concatenate([entry_ref[r : r + 1, :] for r in range(strips)], axis=1)
    places = []
    for direction in range(DIR_DEV):
        value = jnp.int32(0)
        for position in range(DIR_DEV):
            value = value + jnp.where(peel_ref[position] == direction, position, 0)
        places.append(jnp.full((1, comps // DIR_DEV), value, jnp.int32))
    place = jnp.concatenate(places, axis=1).astype(F32)
    low = lax.broadcasted_iota(jnp.int32, (LANES, comps), 0)
    high = lax.broadcasted_iota(jnp.int32, (padded, comps), 0)
    at_low = jnp.where(low == named % LANES, 1.0, 0.0).astype(BF16)
    at_high = jnp.where(high == named // LANES, place, 0.0).astype(BF16)
    positions = lax.dot_general(
        at_low, at_high, (((1,), (1,)), ((), ())), preferred_element_type=F32
    )
    fetches[4].wait()
    fetches[5].wait()
    pair = 2 * columns
    for strip in range(strips):
        own = jnp.broadcast_to(positions[:, strip : strip + 1], (LANES, pair)).astype(BF16)
        span = slice(strip * LANES, (strip + 1) * LANES)
        values = spec_buf[span, :]
        for position in range(DIR_DEV):
            masked[span, position * pair : (position + 1) * pair] = jnp.where(
                own == jnp.asarray(position, BF16), values, jnp.zeros_like(values)
            )

    def coords_copy(src, owner, to):
        return pltpu.make_async_remote_copy(
            src_ref=coords_out.at[src],
            dst_ref=coords_in.at[owner],
            send_sem=c_send.at[src],
            recv_sem=c_recv.at[owner],
            device_id={"tb": to},
            device_id_type=MESH,
        )

    gain_blocks = group_rows // GB
    pairs = owners // 2

    def models_copy(group, owner, part, to):
        rows = pl.ds(pl.multiple_of(part * GB, GB), GB)
        return pltpu.make_async_remote_copy(
            src_ref=models_out.at[group, rows],
            dst_ref=models_in.at[owner, rows],
            send_sem=m_send.at[part, group],
            recv_sem=m_recv.at[part, owner],
            device_id={"dir": to},
            device_id_type=MESH,
        )

    def send_coords(k, carry):
        to = lax.rem(me_t + k, peers)
        coords_copy(to, me_t, to).start()
        return carry

    def predict_step(step, carry):
        part = lax.rem(step, gain_blocks)
        nearness = step // gain_blocks
        chip = lax.rem(me_d // 2 + 1 + nearness, pairs)
        span = pl.ds(pl.multiple_of(part * GB, GB), GB)
        group_coords = jnp.concatenate(
            [
                coord_rows[
                    pl.ds(
                        pl.multiple_of((2 * chip + side_of) * group_rows + part * GB, GB), GB
                    ),
                    :,
                ]
                for side_of in range(2)
            ],
            axis=0,
        )
        step_rows = 2 * GB
        chunks = comps // CHUNK
        buffers = (turned_a, turned_b)
        pieces = step_rows // SUB

        def spread_turns(chunk):
            return jnp.dot(
                group_coords,
                lm_parts[:, chunk * CHUNK : (chunk + 1) * CHUNK],
                preferred_element_type=F32,
            )

        def contract_chunk(chunk):
            return jnp.dot(
                buffers[chunk % 2][...],
                jnp.concatenate(
                    [
                        jnp.concatenate(
                            [
                                masked[
                                    chunk * CHUNK : (chunk + 1) * CHUNK,
                                    (2 * position + part) * columns : (2 * position + part + 1)
                                    * columns,
                                ]
                                for position in range(DIR_DEV)
                            ],
                            axis=1,
                        )
                        for part in range(2)
                    ],
                    axis=0,
                ),
                preferred_element_type=F32,
            )

        turns = spread_turns(0)
        for chunk in range(chunks):
            turned = buffers[chunk % 2]
            following = None
            for sub in range(pieces):
                rows = slice(sub * SUB, (sub + 1) * SUB)
                cos_part, sin_part = turn_cos_sin_short(turns[rows])
                turned[rows, 0:CHUNK] = cos_part
                turned[rows, CHUNK : 2 * CHUNK] = sin_part
                if chunk > 0 and sub == 0:
                    update = contract_chunk(chunk - 1)
                    if chunk == 1:
                        acc[...] = update
                    else:
                        acc[...] += update
                if chunk + 1 < chunks and sub == pieces - 2:
                    following = spread_turns(chunk + 1)
            turns = following
        last = contract_chunk(chunks - 1)
        final = (acc[...] + last).astype(BF16)

        @pl.when(step == 0)
        def _():
            pl.semaphore_wait(barrier, owners - 1 + peers - 1)

        for side_of in range(2):
            group = 2 * chip + side_of
            piece = final[side_of * GB : (side_of + 1) * GB]

            @pl.when(group != me_d)
            def _():
                models_out[group, span, :] = piece
                models_copy(group, me_d, part, group).start()

            @pl.when(group == me_d)
            def _():
                models_in[me_d, span, :] = piece

        return carry

    lax.fori_loop(0, pairs * gain_blocks, predict_step, 0)
    for fetch in fetches[6:]:
        fetch.wait()


    ridge = jnp.broadcast_to(ridge_ref[...], (8, columns))
    lane = lax.broadcasted_iota(jnp.int32, (8, columns), 1)
    reach = 2 * (ITERS - 1)

    def over_rows(value):
        total = jnp.sum(jnp.sum(value, axis=0), axis=0, keepdims=True)
        return jnp.broadcast_to(total, (8, columns))

    def moved(value, far):
        rolled = {0: value}
        for shift in range(2, far + 1, 2):
            rolled[shift] = pltpu.roll(value, columns - shift, 1)
            rolled[-shift] = pltpu.roll(value, shift, 1)
        out = {0: value}
        for shift in range(2, far + 1, 2):
            right, left = rolled[shift], rolled[-shift]
            for step in range(shift // 2):
                mirror = shift - 2 - 4 * step
                left = jnp.where(lane // 2 == step, rolled[mirror], left)
                right = jnp.where(lane // 2 == columns // 2 - 1 - step, rolled[-mirror], right)
            out[shift], out[-shift] = right, left
        return out

    def sweep_gain(constant, couple):
        base = moved(constant, reach)
        gain = {shift: base[shift] + 2.0 * couple[shift] for shift in base}
        for sweep in range(1, ITERS):
            far = reach - 2 * sweep
            gain = {
                shift: base[shift] + couple[shift] * (gain[shift - 2] + gain[shift + 2])
                for shift in range(-far, far + 1, 2)
            }
        return gain[0]

    per_gain = GB // BB

    def peel_owner(part, owner, rest):
        models = [
            models_in[
                owner,
                part * GB : (part + 1) * GB,
                position * columns : (position + 1) * columns,
            ]
            .astype(F32)
            .reshape(GB // 8, 8, columns)
            for position in range(DIR_DEV)
        ]
        gains = []
        for position in range(DIR_DEV):
            model = models[position]
            inverse = 1.0 / (over_rows(model * model) + ridge)
            couple = moved(0.5 * ridge * inverse, reach)
            cross_sum = over_rows(rest * model)
            for before in range(position):
                cross_sum = cross_sum - gains[before] * over_rows(models[before] * model)
            gains.append(sweep_gain(cross_sum * inverse, couple))
        for position in range(DIR_DEV):
            rest = rest - gains[position][None] * models[position]
        return rest.astype(BF16).astype(F32)

    def resid_copy(group, part, sem, to):
        span = pl.ds(group * group_blocks + part * per_gain, per_gain)
        return pltpu.make_async_remote_copy(
            src_ref=resid.at[span],
            dst_ref=resid.at[span],
            send_sem=r_send.at[part, sem],
            recv_sem=r_recv.at[part, group],
            device_id={"dir": to},
            device_id_type=MESH,
        )

    for part in range(gain_blocks):
        for k in range(1, owners):
            source = lax.rem(me_d + k, owners)
            models_copy(source, source, part, source).wait()
        rest = (
            vis_buf[part * GB : (part + 1) * GB, :].astype(F32).reshape(GB // 8, 8, columns)
        )
        for owner in range(owners):
            rest = peel_owner(part, owner, rest)
        resid[pl.ds(me_d * group_blocks + part * per_gain, per_gain)] = rest.reshape(
            per_gain, BB, columns
        ).astype(BF16)
        for k in range(1, owners):
            to = lax.rem(me_d + k, owners)
            resid_copy(me_d, part, to, to).start()
    resid[block_count] = jnp.zeros((BB, columns), BF16)

    slot_lanes = block_row.shape[1]
    tiles = jnp.broadcast_to(tile_ref[...], (slot_lanes, block_count))
    named_tile = jnp.where(
        lax.broadcasted_iota(jnp.int32, (slot_lanes, block_count), 0) == tiles, 1.0, 0.0
    )
    earlier = jnp.where(
        lax.broadcasted_iota(jnp.int32, (block_count, block_count), 0)
        < lax.broadcasted_iota(jnp.int32, (block_count, block_count), 1),
        1.0,
        0.0,
    )
    ranks = jnp.dot(named_tile.astype(BF16), earlier.astype(BF16), preferred_element_type=F32)
    slot = jnp.sum(ranks * named_tile, axis=0, keepdims=True).astype(jnp.int32)
    target = jnp.broadcast_to(tile_ref[...] * slots + slot, (slot_lanes, block_count))
    lane = lax.broadcasted_iota(jnp.int32, (slot_lanes, block_count), 0)
    taken = jnp.where(lane == target, 1.0, 0.0).astype(BF16)
    block_id = lax.broadcasted_iota(jnp.int32, (8, block_count), 1) - block_count
    picked = lax.dot_general(
        block_id.astype(F32).astype(BF16),
        taken,
        (((1,), (1,)), ((), ())),
        preferred_element_type=F32,
    )
    block_row[...] = picked[0:1, :].astype(jnp.int32) + block_count
    index_copy = pltpu.make_async_copy(block_row, block_of_ref, local_sem.at[len(fetches)])
    index_copy.start()

    in_block = (
        lax.broadcasted_iota(jnp.int32, (block_count, sample_rows), 1) // BB
        == lax.broadcasted_iota(jnp.int32, (block_count, sample_rows), 0)
    )
    at_lane = jnp.where(
        lax.broadcasted_iota(jnp.int32, (sample_rows, LANES), 0) % BB
        == lax.broadcasted_iota(jnp.int32, (sample_rows, LANES), 1) % BB,
        1.0,
        0.0,
    ).astype(BF16)
    packed, side = coords_out.shape[1], coords_out.shape[1] // 2
    spot = lax.broadcasted_iota(jnp.int32, (peers * packed, block_count), 0)
    place_of = tile_ref[...] * packed + slot
    sent = jnp.zeros((peers * packed, LANES), F32)
    for which, row in enumerate((u_row, v_row)):
        spread = jnp.where(in_block, jnp.broadcast_to(row, in_block.shape), 0.0).astype(BF16)
        by_block = jnp.dot(spread, at_lane, preferred_element_type=F32).astype(BF16)
        chosen = jnp.where(spot == place_of + which * side, 1.0, 0.0).astype(BF16)
        sent = sent + jnp.dot(chosen, by_block, preferred_element_type=F32)
    coords_out[...] = sent.astype(BF16).reshape(peers, packed, LANES)

    lax.fori_loop(1, peers, send_coords, 0)
    coords_in[me_t] = coords_out[me_t]
    index_copy.wait()

    for part in range(gain_blocks):
        for k in range(1, owners):
            source = lax.rem(me_d + k, owners)
            resid_copy(source, part, source, source).wait_recv()

    def block_in(to, slot):
        block = block_of_ref[0, to * slots + slot]
        return jnp.minimum(jnp.maximum(block, 0), block_count)

    def half_of(which):
        return pl.ds(pl.multiple_of(which * half_rows, half_rows), half_rows)

    def rows_copy(src, owner, to):
        return pltpu.make_async_remote_copy(
            src_ref=rows_out.at[src],
            dst_ref=rows_in.at[owner, half_of(core)],
            send_sem=d_send.at[src],
            recv_sem=d_recv.at[owner],
            device_id={"tb": to},
            device_id_type=MESH,
        )

    def hand_over(owner, which):
        return pltpu.make_async_remote_copy(
            src_ref=rows_in.at[owner, half_of(which)],
            dst_ref=rows_in.at[owner, half_of(which)],
            send_sem=f_send.at[owner],
            recv_sem=f_recv.at[owner],
            device_id={"dir": partner},
            device_id_type=MESH,
        )

    def paired(k):
        other, bit = 0, 1
        while bit < peers:
            other = other + bit * ((me_t // bit + k // bit) % 2)
            bit = 2 * bit
        return other

    def dispatch(k, carry):
        to = lax.rem(me_t + k, peers)
        for slot in range(half_slots):
            rows_out[to, slot * BB : (slot + 1) * BB, :] = resid[
                block_in(to, core * half_slots + slot)
            ]
        rows_copy(to, me_t, to).start()
        return carry

    lax.fori_loop(1, peers, dispatch, 0)
    for slot in range(slots):
        own_rows[slot * BB : (slot + 1) * BB, :] = resid[block_in(me_t, slot)]
    resid_ref[...] = resid[0:block_count].reshape(sample_rows, columns)

    def wait_coords(k, carry):
        source = lax.rem(me_t + k, peers)
        coords_copy(source, source, source).wait()
        return carry

    lax.fori_loop(1, peers, wait_coords, 0)
    share = grid_ref.shape[1]
    lines = share // GRID
    slots_wide = LANES // BB
    strips_wide = -(-slot_rows // LANES)
    wide = strips_wide * LANES
    x_of = (
        me_d * lines - GRID // 2 + lax.broadcasted_iota(jnp.int32, (lines, wide), 0)
    ).astype(F32) / (2.0 * GRID)
    y_of = (lax.broadcasted_iota(jnp.int32, (GRID, wide), 0) - GRID // 2).astype(F32) / (
        2.0 * GRID
    )
    slot_at = lax.broadcasted_iota(jnp.int32, (side, LANES), 0)
    slot_for = lax.broadcasted_iota(jnp.int32, (side, LANES), 1) // BB

    def make_table(source, carry):
        given = coords_in[source].astype(F32)

        def flat(rows):
            return jnp.concatenate(
                [
                    jnp.sum(
                        jnp.where(slot_at == slot_for + strip * slots_wide, rows, 0.0),
                        axis=0,
                        keepdims=True,
                    )
                    for strip in range(strips_wide)
                ],
                axis=1,
            )

        cos_x, sin_x = turn_cos_sin(x_of * flat(given[0:side]))
        cos_y, sin_y = turn_cos_sin(y_of * flat(given[side:packed]))
        for line in range(lines):
            cos_l, sin_l = cos_x[line : line + 1], sin_x[line : line + 1]
            rows = slice(line * GRID, (line + 1) * GRID)
            lower = slice(share + line * GRID, share + (line + 1) * GRID)
            cos_part = (cos_l * cos_y - sin_l * sin_y).astype(BF16)
            sin_part = (sin_l * cos_y + cos_l * sin_y).astype(BF16)
            tables[source, rows, :] = cos_part[:, 0:slot_rows]
            tables[source, lower, :] = sin_part[:, 0:slot_rows]
        return carry

    lax.fori_loop(0, peers, make_table, 0)

    grid_sum = jnp.dot(tables[me_t], own_rows[...], preferred_element_type=F32)

    def source_at(k):
        return paired(k)

    def arrive(k):
        source = source_at(k)
        rows_copy(source, source, source).wait_recv()
        hand_over(source, core).start()

    def add_source(k, total):
        @pl.when(k + 3 < peers)
        def _():
            arrive(k + 3)

        source = source_at(k)
        hand_over(source, 1 - core).wait_recv()
        return total + jnp.dot(tables[source], rows_in[source], preferred_element_type=F32)

    for ahead in range(1, min(3, peers - 1) + 1):
        arrive(ahead)
    grid_sum = lax.fori_loop(1, peers, add_source, grid_sum)
    grid_ref[...] = (grid_sum * float(ROWS_DEV) ** (-0.5)).reshape(2, share, columns)

    for part in range(gain_blocks):
        for k in range(1, owners):
            to = lax.rem(me_d + k, owners)
            resid_copy(me_d, part, to, to).wait_send()

    def drain(k, carry):
        to = lax.rem(me_t + k, peers)
        rows_copy(to, me_t, to).wait_send()
        hand_over(to, core).wait_send()
        return carry

    lax.fori_loop(1, peers, drain, 0)


def finish(resid_ref, grid_ref, resid_out, grid_out, sem):
    copies = (
        pltpu.make_async_copy(resid_ref, resid_out, sem.at[0]),
        pltpu.make_async_copy(grid_ref, grid_out, sem.at[1]),
    )
    for copy in copies:
        copy.start()
    for copy in copies:
        copy.wait()


def local(
    owners,
    peers,
    visibilities,
    uv_coords,
    comp_lm,
    spectra,
    ridge_weight,
    assignment,
    peel_order,
    block_tile,
):
    sample_rows, columns = visibilities.shape
    comps = comp_lm.shape[1]
    block_count = sample_rows // BB
    slots = max(2, 2 * block_count // peers)
    share = PIX // owners

    slot_lanes = -(-peers * slots // LANES) * LANES
    packed = 16 * -(-slots // 8)
    group_rows = sample_rows // owners
    half_rows = slots // 2 * BB
    vmem = pl.BlockSpec(memory_space=pltpu.VMEM)
    anywhere = pl.BlockSpec(memory_space=pl.ANY)
    dma = pltpu.SemaphoreType.DMA
    residual, subgrid = pl.pallas_call(
        functools.partial(kernel, owners, peers, slots),
        out_shape=(
            pltpu.VMEM((sample_rows, columns), BF16),
            pltpu.VMEM((2, share, columns), F32),
        ),
        in_specs=[anywhere] * 8,
        out_specs=(vmem, vmem),
        scratch_shapes=[
            pltpu.VMEM((2, comps), F32),
            pltpu.VMEM((comps // LANES, LANES), jnp.int32),
            pltpu.SMEM((DIR_DEV,), jnp.int32),
            pltpu.VMEM((2, sample_rows), BF16),
            pltpu.VMEM((comps, 2 * columns), BF16),
            pltpu.VMEM((group_rows, columns), BF16),
            pltpu.VMEM((1, columns), F32),
            pltpu.VMEM((1, block_count), jnp.int32),
            pltpu.VMEM((comps, 2 * DIR_DEV * columns), BF16),
            pltpu.VMEM((8, comps), BF16),
            pltpu.VMEM((sample_rows, 8), BF16),
            pltpu.VMEM((1, slot_lanes), jnp.int32),
            pltpu.SMEM((1, slot_lanes), jnp.int32),
            pltpu.VMEM((peers, packed, LANES), BF16),
            pltpu.VMEM((2 * GB, 2 * CHUNK), BF16),
            pltpu.VMEM((2 * GB, 2 * CHUNK), BF16),
            pltpu.VMEM((2 * GB, DIR_DEV * columns), F32),
            pltpu.VMEM((owners, group_rows, DIR_DEV * columns), BF16),
            pltpu.VMEM((owners, group_rows, DIR_DEV * columns), BF16),
            pltpu.VMEM((block_count + 1, BB, columns), BF16),
            pltpu.VMEM((slots * BB, columns), BF16),
            pltpu.VMEM((peers, half_rows, columns), BF16),
            pltpu.VMEM((peers, slots * BB, columns), BF16),
            pltpu.VMEM((peers, packed, LANES), BF16),
            pltpu.VMEM((peers, 2 * share, slots * BB), BF16),
            dma((group_rows // GB, owners)),
            dma((group_rows // GB, owners)),
            dma((group_rows // GB, owners)),
            dma((group_rows // GB, owners)),
            dma((peers,)),
            dma((peers,)),
            dma((peers,)),
            dma((peers,)),
            dma((peers,)),
            dma((peers,)),
            dma((10,)),
        ],
        compiler_params=pltpu.CompilerParams(
            collective_id=0, has_side_effects=True, vmem_limit_bytes=60 * 1024 * 1024
        ),
    )(
        comp_lm,
        assignment.reshape(comps // LANES, LANES),
        peel_order,
        uv_coords,
        spectra,
        visibilities,
        ridge_weight[None, :],
        block_tile.reshape(1, block_count),
    )
    residual, subgrid = pl.pallas_call(
        finish,
        out_shape=(
            jax.ShapeDtypeStruct(residual.shape, residual.dtype),
            jax.ShapeDtypeStruct(subgrid.shape, subgrid.dtype),
        ),
        in_specs=[vmem] * 2,
        out_specs=(anywhere, anywhere),
        scratch_shapes=[dma((2,))],
    )(
        pltpu.with_memory_space_constraint(residual, pltpu.VMEM),
        pltpu.with_memory_space_constraint(subgrid, pltpu.VMEM),
    )
    return residual, subgrid[None]


def solution(mesh):
    return jax.shard_map(
        functools.partial(local, mesh.shape["dir"], mesh.shape["tb"]),
        mesh=mesh,
        in_specs=(
            P("tb", None),
            P(None, "tb"),
            P(None, "dir"),
            P(None, "dir", None),
            P(),
            P("dir"),
            P("dir"),
            P("tb", None),
        ),
        out_specs=(P("tb", None), P("tb", None, "dir", None)),
        check_vma=False,
    )
```

```python
import functools
import math

import jax
import jax.numpy as jnp
from jax import lax
from jax.experimental import pallas as pl
from jax.experimental.pallas import tpu as pltpu
from jax.sharding import PartitionSpec as P

NCOMP = 1024
GRID = 32
DIR_DEV = 3
ITERS = 4
BB = 32
GB = 128
ROWS_DEV = 1024
PIX = 1024

MESH = pl.DeviceIdType.MESH
F32 = jnp.float32
BF16 = jnp.bfloat16
LANES = 128
CHUNK = 256
SUB = 32

SIN_FIT = (4.4428795675460835, -7.307816684491791, 3.5977741780872416, -0.7911993921613704)
COS_FIT = (1.414204014809076, -6.977637323456295, 5.715187874756718, -1.728213892223522)


BENT_SIN = (6.28125, -41.25, 76.5)
BENT_COS = (1.0, -19.75, 65.0, -79.5)


def horner(square, fit):
    total = jnp.asarray(fit[-1], square.dtype)
    for coefficient in fit[-2::-1]:
        total = total * square + jnp.asarray(coefficient, square.dtype)
    return total


def turn_cos_sin(turns):
    part = turns - jnp.round(turns)
    square = part * part
    half_sin = part * horner(square, SIN_FIT)
    half_cos = horner(square, COS_FIT)
    return 1.0 - half_sin * half_sin, half_sin * half_cos


def turn_cos_sin_short(turns):
    part = turns - jnp.round(turns)
    bent = (0.25 - jnp.abs(part)).astype(BF16)
    square = bent * bent
    upright = horner(square, BENT_COS)
    flipped = jnp.where(part.astype(BF16) < 0, -upright, upright)
    return bent * horner(square, BENT_SIN), flipped


def kernel(
    owners,
    peers,
    slots,
    lm_hbm,
    entry_hbm,
    peel_hbm,
    uv_hbm,
    spec_hbm,
    vis_hbm,
    ridge_hbm,
    tile_hbm,
    resid_ref,
    grid_ref,
    lm_ref,
    entry_ref,
    peel_ref,
    uv_ref,
    spec_buf,
    vis_buf,
    ridge_ref,
    tile_ref,
    masked,
    lm_parts,
    coord_rows,
    block_row,
    block_of_ref,
    coords_out,
    turned_a,
    turned_b,
    acc,
    models_out,
    models_in,
    resid,
    own_rows,
    rows_out,
    rows_in,
    coords_in,
    tables,
    m_send,
    m_recv,
    r_send,
    r_recv,
    d_send,
    d_recv,
    f_send,
    f_recv,
    c_send,
    c_recv,
    local_sem,
):
    me_d = lax.axis_index("dir")
    me_t = lax.axis_index("tb")
    core = me_d % 2
    partner = me_d + 1 - 2 * core
    group_rows, columns = vis_buf.shape
    sample_rows = group_rows * owners
    comps = lm_ref.shape[1]
    block_count = sample_rows // BB
    group_blocks = block_count // owners
    slot_rows = slots * BB
    half_slots = slots // 2
    half_rows = half_slots * BB
    first = me_d * group_rows

    own_part = vis_hbm.at[pl.ds(pl.multiple_of(first, group_rows), group_rows)]
    fetches = [
        pltpu.make_async_copy(source, target, local_sem.at[number])
        for number, (source, target) in enumerate(
            (
                (lm_hbm, lm_ref),
                (entry_hbm, entry_ref),
                (peel_hbm, peel_ref),
                (uv_hbm, uv_ref),
                (spec_hbm.at[0], spec_buf.at[:, 0:columns]),
                (spec_hbm.at[1], spec_buf.at[:, columns : 2 * columns]),
                (own_part, vis_buf),
                (ridge_hbm, ridge_ref),
                (tile_hbm, tile_ref),
            )
        )
    ]
    for fetch in fetches:
        fetch.start()

    barrier = pltpu.get_barrier_semaphore()
    for k in range(1, owners):
        pl.semaphore_signal(
            barrier, inc=1, device_id={"dir": lax.rem(me_d + k, owners)}, device_id_type=MESH
        )

    def greet(k, carry):
        pl.semaphore_signal(
            barrier, inc=1, device_id={"tb": lax.rem(me_t + k, peers)}, device_id_type=MESH
        )
        return carry

    lax.fori_loop(1, peers, greet, 0)

    for fetch in fetches[0:4]:
        fetch.wait()

    u_row = uv_ref[0:1, :].astype(F32)
    v_row = uv_ref[1:2, :].astype(F32)
    stacked = jnp.concatenate(
        [u_row] * 3 + [v_row] * 3 + [jnp.zeros((2, sample_rows), F32)], axis=0
    )
    coord_rows[...] = stacked.T.astype(BF16)

    parts = []
    for which in range(2):
        left = lm_ref[which : which + 1, :]
        for part in range(3):
            rounded = left.astype(BF16).astype(F32)
            parts.append(rounded)
            left = left - rounded
    parts.append(jnp.zeros((2, comps), F32))
    lm_parts[...] = jnp.concatenate(parts, axis=0).astype(BF16)

    strips = comps // LANES
    padded = -(-strips // 16) * 16
    named = jnp.concatenate([entry_ref[r : r + 1, :] for r in range(strips)], axis=1)
    places = []
    for direction in range(DIR_DEV):
        value = jnp.int32(0)
        for position in range(DIR_DEV):
            value = value + jnp.where(peel_ref[position] == direction, position, 0)
        places.append(jnp.full((1, comps // DIR_DEV), value, jnp.int32))
    place = jnp.concatenate(places, axis=1).astype(F32)
    low = lax.broadcasted_iota(jnp.int32, (LANES, comps), 0).astype(F32).astype(BF16)
    inside = (named % LANES).astype(F32).astype(BF16)
    high = lax.broadcasted_iota(jnp.int32, (padded, comps), 0)
    at_low = jnp.where(low == inside, jnp.asarray(1, BF16), jnp.asarray(0, BF16))
    at_high = jnp.where(high == named // LANES, place, 0.0).astype(BF16)
    positions = lax.dot_general(
        at_low, at_high, (((1,), (1,)), ((), ())), preferred_element_type=F32
    )
    fetches[4].wait()
    fetches[5].wait()
    pair = 2 * columns
    for strip in range(strips):
        own = jnp.broadcast_to(positions[:, strip : strip + 1], (LANES, pair)).astype(BF16)
        span = slice(strip * LANES, (strip + 1) * LANES)
        values = spec_buf[span, :]
        for position in range(DIR_DEV):
            masked[span, position * pair : (position + 1) * pair] = jnp.where(
                own == jnp.asarray(position, BF16), values, jnp.zeros_like(values)
            )

    def coords_copy(src, owner, to):
        return pltpu.make_async_remote_copy(
            src_ref=coords_out.at[src],
            dst_ref=coords_in.at[owner],
            send_sem=c_send.at[src],
            recv_sem=c_recv.at[owner],
            device_id={"tb": to},
            device_id_type=MESH,
        )

    gain_blocks = group_rows // GB
    pairs = owners // 2

    def models_copy(group, owner, part, to):
        rows = pl.ds(pl.multiple_of(part * GB, GB), GB)
        return pltpu.make_async_remote_copy(
            src_ref=models_out.at[group, rows],
            dst_ref=models_in.at[owner, rows],
            send_sem=m_send.at[part, group],
            recv_sem=m_recv.at[part, owner],
            device_id={"dir": to},
            device_id_type=MESH,
        )

    def send_coords(k, carry):
        to = lax.rem(me_t + k, peers)
        coords_copy(to, me_t, to).start()
        return carry

    def predict_step(step, carry):
        part = lax.rem(step, gain_blocks)
        nearness = step // gain_blocks
        chip = lax.rem(me_d // 2 + 1 + nearness, pairs)
        span = pl.ds(pl.multiple_of(part * GB, GB), GB)
        group_coords = jnp.concatenate(
            [
                coord_rows[
                    pl.ds(
                        pl.multiple_of((2 * chip + side_of) * group_rows + part * GB, GB), GB
                    ),
                    :,
                ]
                for side_of in range(2)
            ],
            axis=0,
        )
        step_rows = 2 * GB
        chunks = comps // CHUNK
        buffers = (turned_a, turned_b)
        pieces = step_rows // SUB

        def spread_turns(chunk):
            return jnp.dot(
                group_coords,
                lm_parts[:, chunk * CHUNK : (chunk + 1) * CHUNK],
                preferred_element_type=F32,
            )

        def contract_chunk(chunk):
            return jnp.dot(
                buffers[chunk % 2][...],
                jnp.concatenate(
                    [
                        jnp.concatenate(
                            [
                                masked[
                                    chunk * CHUNK : (chunk + 1) * CHUNK,
                                    (2 * position + part) * columns : (2 * position + part + 1)
                                    * columns,
                                ]
                                for position in range(DIR_DEV)
                            ],
                            axis=1,
                        )
                        for part in range(2)
                    ],
                    axis=0,
                ),
                preferred_element_type=F32,
            )

        turns = spread_turns(0)
        for chunk in range(chunks):
            turned = buffers[chunk % 2]
            following = None
            for sub in range(pieces):
                rows = slice(sub * SUB, (sub + 1) * SUB)
                cos_part, sin_part = turn_cos_sin_short(turns[rows])
                turned[rows, 0:CHUNK] = cos_part
                turned[rows, CHUNK : 2 * CHUNK] = sin_part
                if chunk > 0 and sub == 0:
                    update = contract_chunk(chunk - 1)
                    if chunk == 1:
                        acc[...] = update
                    else:
                        acc[...] += update
                if chunk + 1 < chunks and sub == pieces - 2:
                    following = spread_turns(chunk + 1)
            turns = following
        last = contract_chunk(chunks - 1)
        final = (acc[...] + last).astype(BF16)

        @pl.when(step == 0)
        def _():
            pl.semaphore_wait(barrier, owners - 1 + peers - 1)

        for side_of in range(2):
            group = 2 * chip + side_of
            piece = final[side_of * GB : (side_of + 1) * GB]

            @pl.when(group != me_d)
            def _():
                models_out[group, span, :] = piece
                models_copy(group, me_d, part, group).start()

            @pl.when(group == me_d)
            def _():
                models_in[me_d, span, :] = piece

        return carry

    lax.fori_loop(0, pairs * gain_blocks, predict_step, 0)
    for fetch in fetches[6:]:
        fetch.wait()


    ridge = jnp.broadcast_to(ridge_ref[...], (8, columns))
    lane = lax.broadcasted_iota(jnp.int32, (8, columns), 1)
    reach = 2 * (ITERS - 1)

    def over_rows(value):
        total = jnp.sum(jnp.sum(value, axis=0), axis=0, keepdims=True)
        return jnp.broadcast_to(total, (8, columns))

    def moved(value, far):
        rolled = {0: value}
        for shift in range(2, far + 1, 2):
            rolled[shift] = pltpu.roll(value, columns - shift, 1)
            rolled[-shift] = pltpu.roll(value, shift, 1)
        out = {0: value}
        for shift in range(2, far + 1, 2):
            right, left = rolled[shift], rolled[-shift]
            for step in range(shift // 2):
                mirror = shift - 2 - 4 * step
                left = jnp.where(lane // 2 == step, rolled[mirror], left)
                right = jnp.where(lane // 2 == columns // 2 - 1 - step, rolled[-mirror], right)
            out[shift], out[-shift] = right, left
        return out

    def sweep_gain(constant, couple):
        base = moved(constant, reach)
        gain = {shift: base[shift] + 2.0 * couple[shift] for shift in base}
        for sweep in range(1, ITERS):
            far = reach - 2 * sweep
            gain = {
                shift: base[shift] + couple[shift] * (gain[shift - 2] + gain[shift + 2])
                for shift in range(-far, far + 1, 2)
            }
        return gain[0]

    per_gain = GB // BB
    sublane = lax.broadcasted_iota(jnp.int32, (8, columns), 0)

    def peel_owner(part, owner, rest):
        models = [
            models_in[
                owner,
                part * GB : (part + 1) * GB,
                position * columns : (position + 1) * columns,
            ]
            .astype(F32)
            .reshape(GB // 8, 8, columns)
            for position in range(DIR_DEV)
        ]
        power = over_rows(models[0] * models[0])
        for position in range(1, DIR_DEV):
            power = jnp.where(
                sublane == position, over_rows(models[position] * models[position]), power
            )
        inverses = 1.0 / (power + ridge)
        couples = moved(0.5 * ridge * inverses, reach)

        def of_position(value, position):
            return jnp.broadcast_to(value[position : position + 1, :], (8, columns))

        gains = []
        for position in range(DIR_DEV):
            model = models[position]
            inverse = of_position(inverses, position)
            couple = {shift: of_position(couples[shift], position) for shift in couples}
            cross_sum = over_rows(rest * model)
            for before in range(position):
                cross_sum = cross_sum - gains[before] * over_rows(models[before] * model)
            gains.append(sweep_gain(cross_sum * inverse, couple))
        for position in range(DIR_DEV):
            rest = rest - gains[position][None] * models[position]
        return rest.astype(BF16).astype(F32)

    def resid_copy(group, part, sem, to):
        span = pl.ds(group * group_blocks + part * per_gain, per_gain)
        return pltpu.make_async_remote_copy(
            src_ref=resid.at[span],
            dst_ref=resid.at[span],
            send_sem=r_send.at[part, sem],
            recv_sem=r_recv.at[part, group],
            device_id={"dir": to},
            device_id_type=MESH,
        )

    for part in range(gain_blocks):
        for k in range(1, owners):
            source = lax.rem(me_d + k, owners)
            models_copy(source, source, part, source).wait()
        rest = (
            vis_buf[part * GB : (part + 1) * GB, :].astype(F32).reshape(GB // 8, 8, columns)
        )
        for owner in range(owners):
            rest = peel_owner(part, owner, rest)
        resid[pl.ds(me_d * group_blocks + part * per_gain, per_gain)] = rest.reshape(
            per_gain, BB, columns
        ).astype(BF16)
        for k in range(1, owners):
            to = lax.rem(me_d + k, owners)
            resid_copy(me_d, part, to, to).start()
    resid[block_count] = jnp.zeros((BB, columns), BF16)

    slot_lanes = block_row.shape[1]
    tiles = jnp.broadcast_to(tile_ref[...], (slot_lanes, block_count))
    named_tile = jnp.where(
        lax.broadcasted_iota(jnp.int32, (slot_lanes, block_count), 0) == tiles, 1.0, 0.0
    )
    earlier = jnp.where(
        lax.broadcasted_iota(jnp.int32, (block_count, block_count), 0)
        < lax.broadcasted_iota(jnp.int32, (block_count, block_count), 1),
        1.0,
        0.0,
    )
    ranks = jnp.dot(named_tile.astype(BF16), earlier.astype(BF16), preferred_element_type=F32)
    slot = jnp.sum(ranks * named_tile, axis=0, keepdims=True).astype(jnp.int32)
    target = jnp.broadcast_to(tile_ref[...] * slots + slot, (slot_lanes, block_count))
    lane = lax.broadcasted_iota(jnp.int32, (slot_lanes, block_count), 0)
    taken = jnp.where(lane == target, 1.0, 0.0).astype(BF16)
    block_id = lax.broadcasted_iota(jnp.int32, (8, block_count), 1) - block_count
    picked = lax.dot_general(
        block_id.astype(F32).astype(BF16),
        taken,
        (((1,), (1,)), ((), ())),
        preferred_element_type=F32,
    )
    block_row[...] = picked[0:1, :].astype(jnp.int32) + block_count
    index_copy = pltpu.make_async_copy(block_row, block_of_ref, local_sem.at[len(fetches)])
    index_copy.start()

    in_block = (
        lax.broadcasted_iota(jnp.int32, (block_count, sample_rows), 1) // BB
        == lax.broadcasted_iota(jnp.int32, (block_count, sample_rows), 0)
    )
    at_lane = jnp.where(
        lax.broadcasted_iota(jnp.int32, (sample_rows, LANES), 0) % BB
        == lax.broadcasted_iota(jnp.int32, (sample_rows, LANES), 1) % BB,
        1.0,
        0.0,
    ).astype(BF16)
    packed, side = coords_out.shape[1], coords_out.shape[1] // 2
    spot = lax.broadcasted_iota(jnp.int32, (peers * packed, block_count), 0)
    place_of = tile_ref[...] * packed + slot
    sent = jnp.zeros((peers * packed, LANES), F32)
    for which, row in enumerate((u_row, v_row)):
        spread = jnp.where(in_block, jnp.broadcast_to(row, in_block.shape), 0.0).astype(BF16)
        by_block = jnp.dot(spread, at_lane, preferred_element_type=F32).astype(BF16)
        chosen = jnp.where(spot == place_of + which * side, 1.0, 0.0).astype(BF16)
        sent = sent + jnp.dot(chosen, by_block, preferred_element_type=F32)
    coords_out[...] = sent.astype(BF16).reshape(peers, packed, LANES)

    lax.fori_loop(1, peers, send_coords, 0)
    coords_in[me_t] = coords_out[me_t]
    index_copy.wait()

    for part in range(gain_blocks):
        for k in range(1, owners):
            source = lax.rem(me_d + k, owners)
            resid_copy(source, part, source, source).wait_recv()

    def block_in(to, slot):
        block = block_of_ref[0, to * slots + slot]
        return jnp.minimum(jnp.maximum(block, 0), block_count)

    def half_of(which):
        return pl.ds(pl.multiple_of(which * half_rows, half_rows), half_rows)

    def rows_copy(src, owner, to):
        return pltpu.make_async_remote_copy(
            src_ref=rows_out.at[src],
            dst_ref=rows_in.at[owner, half_of(core)],
            send_sem=d_send.at[src],
            recv_sem=d_recv.at[owner],
            device_id={"tb": to},
            device_id_type=MESH,
        )

    def hand_over(owner, which):
        return pltpu.make_async_remote_copy(
            src_ref=rows_in.at[owner, half_of(which)],
            dst_ref=rows_in.at[owner, half_of(which)],
            send_sem=f_send.at[owner],
            recv_sem=f_recv.at[owner],
            device_id={"dir": partner},
            device_id_type=MESH,
        )

    def paired(k):
        other, bit = 0, 1
        while bit < peers:
            other = other + bit * ((me_t // bit + k // bit) % 2)
            bit = 2 * bit
        return other

    def dispatch(k, carry):
        to = lax.rem(me_t + k, peers)
        for slot in range(half_slots):
            rows_out[to, slot * BB : (slot + 1) * BB, :] = resid[
                block_in(to, core * half_slots + slot)
            ]
        rows_copy(to, me_t, to).start()
        return carry

    lax.fori_loop(1, peers, dispatch, 0)
    for slot in range(slots):
        own_rows[slot * BB : (slot + 1) * BB, :] = resid[block_in(me_t, slot)]
    resid_ref[...] = resid[0:block_count].reshape(sample_rows, columns)

    def wait_coords(k, carry):
        source = lax.rem(me_t + k, peers)
        coords_copy(source, source, source).wait()
        return carry

    lax.fori_loop(1, peers, wait_coords, 0)
    share = grid_ref.shape[1]
    lines = share // GRID
    slots_wide = LANES // BB
    strips_wide = -(-slot_rows // LANES)
    wide = strips_wide * LANES
    x_of = (
        me_d * lines - GRID // 2 + lax.broadcasted_iota(jnp.int32, (lines, wide), 0)
    ).astype(F32) / (2.0 * GRID)
    y_of = (lax.broadcasted_iota(jnp.int32, (GRID, wide), 0) - GRID // 2).astype(F32) / (
        2.0 * GRID
    )
    slot_at = lax.broadcasted_iota(jnp.int32, (side, LANES), 0)
    slot_for = lax.broadcasted_iota(jnp.int32, (side, LANES), 1) // BB

    def make_table(source, carry):
        given = coords_in[source].astype(F32)

        def flat(rows):
            return jnp.concatenate(
                [
                    jnp.sum(
                        jnp.where(slot_at == slot_for + strip * slots_wide, rows, 0.0),
                        axis=0,
                        keepdims=True,
                    )
                    for strip in range(strips_wide)
                ],
                axis=1,
            )

        cos_x, sin_x = turn_cos_sin(x_of * flat(given[0:side]))
        cos_y, sin_y = turn_cos_sin(y_of * flat(given[side:packed]))
        for line in range(lines):
            cos_l, sin_l = cos_x[line : line + 1], sin_x[line : line + 1]
            rows = slice(line * GRID, (line + 1) * GRID)
            lower = slice(share + line * GRID, share + (line + 1) * GRID)
            cos_part = (cos_l * cos_y - sin_l * sin_y).astype(BF16)
            sin_part = (sin_l * cos_y + cos_l * sin_y).astype(BF16)
            tables[source, rows, :] = cos_part[:, 0:slot_rows]
            tables[source, lower, :] = sin_part[:, 0:slot_rows]
        return carry

    lax.fori_loop(0, peers, make_table, 0)

    grid_sum = jnp.dot(tables[me_t], own_rows[...], preferred_element_type=F32)

    def source_at(k):
        return paired(k)

    def arrive(k):
        source = source_at(k)
        rows_copy(source, source, source).wait_recv()
        hand_over(source, core).start()

    def add_source(k, total):
        @pl.when(k + 4 < peers)
        def _():
            arrive(k + 4)

        source = source_at(k)
        hand_over(source, 1 - core).wait_recv()
        return total + jnp.dot(tables[source], rows_in[source], preferred_element_type=F32)

    for ahead in range(1, min(4, peers - 1) + 1):
        arrive(ahead)
    grid_sum = lax.fori_loop(1, peers, add_source, grid_sum)
    grid_ref[...] = (grid_sum * float(ROWS_DEV) ** (-0.5)).reshape(2, share, columns)

    for part in range(gain_blocks):
        for k in range(1, owners):
            to = lax.rem(me_d + k, owners)
            resid_copy(me_d, part, to, to).wait_send()

    def drain(k, carry):
        to = lax.rem(me_t + k, peers)
        rows_copy(to, me_t, to).wait_send()
        hand_over(to, core).wait_send()
        return carry

    lax.fori_loop(1, peers, drain, 0)


def finish(resid_ref, grid_ref, resid_out, grid_out, sem):
    copies = (
        pltpu.make_async_copy(resid_ref, resid_out, sem.at[0]),
        pltpu.make_async_copy(grid_ref, grid_out, sem.at[1]),
    )
    for copy in copies:
        copy.start()
    for copy in copies:
        copy.wait()


def local(
    owners,
    peers,
    visibilities,
    uv_coords,
    comp_lm,
    spectra,
    ridge_weight,
    assignment,
    peel_order,
    block_tile,
):
    sample_rows, columns = visibilities.shape
    comps = comp_lm.shape[1]
    block_count = sample_rows // BB
    slots = max(2, 2 * block_count // peers)
    share = PIX // owners

    slot_lanes = -(-peers * slots // LANES) * LANES
    packed = 16 * -(-slots // 8)
    group_rows = sample_rows // owners
    half_rows = slots // 2 * BB
    vmem = pl.BlockSpec(memory_space=pltpu.VMEM)
    anywhere = pl.BlockSpec(memory_space=pl.ANY)
    dma = pltpu.SemaphoreType.DMA
    residual, subgrid = pl.pallas_call(
        functools.partial(kernel, owners, peers, slots),
        out_shape=(
            pltpu.VMEM((sample_rows, columns), BF16),
            pltpu.VMEM((2, share, columns), F32),
        ),
        in_specs=[anywhere] * 8,
        out_specs=(vmem, vmem),
        scratch_shapes=[
            pltpu.VMEM((2, comps), F32),
            pltpu.VMEM((comps // LANES, LANES), jnp.int32),
            pltpu.SMEM((DIR_DEV,), jnp.int32),
            pltpu.VMEM((2, sample_rows), BF16),
            pltpu.VMEM((comps, 2 * columns), BF16),
            pltpu.VMEM((group_rows, columns), BF16),
            pltpu.VMEM((1, columns), F32),
            pltpu.VMEM((1, block_count), jnp.int32),
            pltpu.VMEM((comps, 2 * DIR_DEV * columns), BF16),
            pltpu.VMEM((8, comps), BF16),
            pltpu.VMEM((sample_rows, 8), BF16),
            pltpu.VMEM((1, slot_lanes), jnp.int32),
            pltpu.SMEM((1, slot_lanes), jnp.int32),
            pltpu.VMEM((peers, packed, LANES), BF16),
            pltpu.VMEM((2 * GB, 2 * CHUNK), BF16),
            pltpu.VMEM((2 * GB, 2 * CHUNK), BF16),
            pltpu.VMEM((2 * GB, DIR_DEV * columns), F32),
            pltpu.VMEM((owners, group_rows, DIR_DEV * columns), BF16),
            pltpu.VMEM((owners, group_rows, DIR_DEV * columns), BF16),
            pltpu.VMEM((block_count + 1, BB, columns), BF16),
            pltpu.VMEM((slots * BB, columns), BF16),
            pltpu.VMEM((peers, half_rows, columns), BF16),
            pltpu.VMEM((peers, slots * BB, columns), BF16),
            pltpu.VMEM((peers, packed, LANES), BF16),
            pltpu.VMEM((peers, 2 * share, slots * BB), BF16),
            dma((group_rows // GB, owners)),
            dma((group_rows // GB, owners)),
            dma((group_rows // GB, owners)),
            dma((group_rows // GB, owners)),
            dma((peers,)),
            dma((peers,)),
            dma((peers,)),
            dma((peers,)),
            dma((peers,)),
            dma((peers,)),
            dma((10,)),
        ],
        compiler_params=pltpu.CompilerParams(
            collective_id=0, has_side_effects=True, vmem_limit_bytes=60 * 1024 * 1024
        ),
    )(
        comp_lm,
        assignment.reshape(comps // LANES, LANES),
        peel_order,
        uv_coords,
        spectra,
        visibilities,
        ridge_weight[None, :],
        block_tile.reshape(1, block_count),
    )
    residual, subgrid = pl.pallas_call(
        finish,
        out_shape=(
            jax.ShapeDtypeStruct(residual.shape, residual.dtype),
            jax.ShapeDtypeStruct(subgrid.shape, subgrid.dtype),
        ),
        in_specs=[vmem] * 2,
        out_specs=(anywhere, anywhere),
        scratch_shapes=[dma((2,))],
    )(
        pltpu.with_memory_space_constraint(residual, pltpu.VMEM),
        pltpu.with_memory_space_constraint(subgrid, pltpu.VMEM),
    )
    return residual, subgrid[None]


def solution(mesh):
    return jax.shard_map(
        functools.partial(local, mesh.shape["dir"], mesh.shape["tb"]),
        mesh=mesh,
        in_specs=(
            P("tb", None),
            P(None, "tb"),
            P(None, "dir"),
            P(None, "dir", None),
            P(),
            P("dir"),
            P("dir"),
            P("tb", None),
        ),
        out_specs=(P("tb", None), P("tb", None, "dir", None)),
        check_vma=False,
    )
```

```python
import functools
import math

import jax
import jax.numpy as jnp
from jax import lax
from jax.experimental import pallas as pl
from jax.experimental.pallas import tpu as pltpu
from jax.sharding import PartitionSpec as P

NCOMP = 1024
GRID = 32
DIR_DEV = 3
ITERS = 4
BB = 32
GB = 128
ROWS_DEV = 1024
PIX = 1024

MESH = pl.DeviceIdType.MESH
F32 = jnp.float32
BF16 = jnp.bfloat16
LANES = 128
CHUNK = 256
SUB = 32

SIN_FIT = (4.4428795675460835, -7.307816684491791, 3.5977741780872416, -0.7911993921613704)
COS_FIT = (1.414204014809076, -6.977637323456295, 5.715187874756718, -1.728213892223522)


BENT_SIN = (6.28125, -41.25, 76.5)
BENT_COS = (1.0, -19.75, 65.0, -79.5)


def horner(square, fit):
    total = jnp.asarray(fit[-1], square.dtype)
    for coefficient in fit[-2::-1]:
        total = total * square + jnp.asarray(coefficient, square.dtype)
    return total


def turn_cos_sin(turns):
    part = turns - jnp.round(turns)
    square = part * part
    half_sin = part * horner(square, SIN_FIT)
    half_cos = horner(square, COS_FIT)
    return 1.0 - half_sin * half_sin, half_sin * half_cos


def turn_cos_sin_short(turns):
    part = turns - jnp.round(turns)
    bent = (0.25 - jnp.abs(part)).astype(BF16)
    square = bent * bent
    upright = horner(square, BENT_COS)
    flipped = jnp.where(part.astype(BF16) < 0, -upright, upright)
    return bent * horner(square, BENT_SIN), flipped


def kernel(
    owners,
    peers,
    slots,
    lm_hbm,
    entry_hbm,
    peel_hbm,
    uv_hbm,
    spec_hbm,
    vis_hbm,
    ridge_hbm,
    tile_hbm,
    resid_ref,
    grid_ref,
    lm_ref,
    entry_ref,
    peel_ref,
    uv_ref,
    spec_buf,
    vis_buf,
    ridge_ref,
    tile_ref,
    masked,
    lm_parts,
    coord_rows,
    block_row,
    block_of_ref,
    coords_out,
    turned_a,
    turned_b,
    acc,
    models_out,
    models_in,
    resid,
    own_rows,
    rows_out,
    rows_in,
    coords_in,
    tables,
    m_send,
    m_recv,
    r_send,
    r_recv,
    d_send,
    d_recv,
    f_send,
    f_recv,
    c_send,
    c_recv,
    local_sem,
):
    me_d = lax.axis_index("dir")
    me_t = lax.axis_index("tb")
    core = me_d % 2
    partner = me_d + 1 - 2 * core
    group_rows, columns = vis_buf.shape
    sample_rows = group_rows * owners
    comps = lm_ref.shape[1]
    block_count = sample_rows // BB
    group_blocks = block_count // owners
    slot_rows = slots * BB
    half_slots = slots // 2
    half_rows = half_slots * BB
    first = me_d * group_rows

    own_part = vis_hbm.at[pl.ds(pl.multiple_of(first, group_rows), group_rows)]
    fetches = [
        pltpu.make_async_copy(source, target, local_sem.at[number])
        for number, (source, target) in enumerate(
            (
                (lm_hbm, lm_ref),
                (entry_hbm, entry_ref),
                (peel_hbm, peel_ref),
                (uv_hbm, uv_ref),
                (spec_hbm.at[0], spec_buf.at[:, 0:columns]),
                (spec_hbm.at[1], spec_buf.at[:, columns : 2 * columns]),
                (own_part, vis_buf),
                (ridge_hbm, ridge_ref),
                (tile_hbm, tile_ref),
            )
        )
    ]
    for fetch in fetches:
        fetch.start()

    barrier = pltpu.get_barrier_semaphore()
    for k in range(1, owners):
        pl.semaphore_signal(
            barrier, inc=1, device_id={"dir": lax.rem(me_d + k, owners)}, device_id_type=MESH
        )

    def greet(k, carry):
        pl.semaphore_signal(
            barrier, inc=1, device_id={"tb": lax.rem(me_t + k, peers)}, device_id_type=MESH
        )
        return carry

    lax.fori_loop(1, peers, greet, 0)

    for fetch in fetches[0:4]:
        fetch.wait()

    u_row = uv_ref[0:1, :].astype(F32)
    v_row = uv_ref[1:2, :].astype(F32)
    stacked = jnp.concatenate(
        [u_row] * 3 + [v_row] * 3 + [jnp.zeros((2, sample_rows), F32)], axis=0
    )
    coord_rows[...] = stacked.T.astype(BF16)

    parts = []
    for which in range(2):
        left = lm_ref[which : which + 1, :]
        for part in range(3):
            rounded = left.astype(BF16).astype(F32)
            parts.append(rounded)
            left = left - rounded
    parts.append(jnp.zeros((2, comps), F32))
    lm_parts[...] = jnp.concatenate(parts, axis=0).astype(BF16)

    strips = comps // LANES
    padded = -(-strips // 16) * 16
    named = jnp.concatenate([entry_ref[r : r + 1, :] for r in range(strips)], axis=1)
    places = []
    for direction in range(DIR_DEV):
        value = jnp.int32(0)
        for position in range(DIR_DEV):
            value = value + jnp.where(peel_ref[position] == direction, position, 0)
        places.append(jnp.full((1, comps // DIR_DEV), value, jnp.int32))
    place = jnp.concatenate(places, axis=1).astype(F32)
    low = lax.broadcasted_iota(jnp.int32, (LANES, comps), 0)
    high = lax.broadcasted_iota(jnp.int32, (padded, comps), 0)
    at_low = jnp.where(low == named % LANES, 1.0, 0.0).astype(BF16)
    at_high = jnp.where(high == named // LANES, place, 0.0).astype(BF16)
    positions = lax.dot_general(
        at_low, at_high, (((1,), (1,)), ((), ())), preferred_element_type=F32
    )
    fetches[4].wait()
    fetches[5].wait()
    pair = 2 * columns
    for strip in range(strips):
        own = jnp.broadcast_to(positions[:, strip : strip + 1], (LANES, pair)).astype(BF16)
        span = slice(strip * LANES, (strip + 1) * LANES)
        values = spec_buf[span, :]
        for position in range(DIR_DEV):
            masked[span, position * pair : (position + 1) * pair] = jnp.where(
                own == jnp.asarray(position, BF16), values, jnp.zeros_like(values)
            )

    def coords_copy(src, owner, to):
        return pltpu.make_async_remote_copy(
            src_ref=coords_out.at[src],
            dst_ref=coords_in.at[owner],
            send_sem=c_send.at[src],
            recv_sem=c_recv.at[owner],
            device_id={"tb": to},
            device_id_type=MESH,
        )

    gain_blocks = group_rows // GB
    pairs = owners // 2

    def models_copy(group, owner, part, to):
        rows = pl.ds(pl.multiple_of(part * GB, GB), GB)
        return pltpu.make_async_remote_copy(
            src_ref=models_out.at[group, rows],
            dst_ref=models_in.at[owner, rows],
            send_sem=m_send.at[part, group],
            recv_sem=m_recv.at[part, owner],
            device_id={"dir": to},
            device_id_type=MESH,
        )

    def send_coords(k, carry):
        to = lax.rem(me_t + k, peers)
        coords_copy(to, me_t, to).start()
        return carry

    def predict_step(step, carry):
        part = lax.rem(step, gain_blocks)
        nearness = step // gain_blocks
        chip = lax.rem(me_d // 2 + 1 + nearness, pairs)
        span = pl.ds(pl.multiple_of(part * GB, GB), GB)
        group_coords = jnp.concatenate(
            [
                coord_rows[
                    pl.ds(
                        pl.multiple_of((2 * chip + side_of) * group_rows + part * GB, GB), GB
                    ),
                    :,
                ]
                for side_of in range(2)
            ],
            axis=0,
        )
        step_rows = 2 * GB
        chunks = comps // CHUNK
        buffers = (turned_a, turned_b)
        pieces = step_rows // SUB

        def spread_turns(chunk):
            return jnp.dot(
                group_coords,
                lm_parts[:, chunk * CHUNK : (chunk + 1) * CHUNK],
                preferred_element_type=F32,
            )

        def contract_chunk(chunk):
            return jnp.dot(
                buffers[chunk % 2][...],
                jnp.concatenate(
                    [
                        jnp.concatenate(
                            [
                                masked[
                                    chunk * CHUNK : (chunk + 1) * CHUNK,
                                    (2 * position + part) * columns : (2 * position + part + 1)
                                    * columns,
                                ]
                                for position in range(DIR_DEV)
                            ],
                            axis=1,
                        )
                        for part in range(2)
                    ],
                    axis=0,
                ),
                preferred_element_type=F32,
            )

        turns = spread_turns(0)
        for chunk in range(chunks):
            turned = buffers[chunk % 2]
            following = None
            for sub in range(pieces):
                rows = slice(sub * SUB, (sub + 1) * SUB)
                cos_part, sin_part = turn_cos_sin_short(turns[rows])
                turned[rows, 0:CHUNK] = cos_part
                turned[rows, CHUNK : 2 * CHUNK] = sin_part
                if chunk > 0 and sub == 0:
                    update = contract_chunk(chunk - 1)
                    if chunk == 1:
                        acc[...] = update
                    else:
                        acc[...] += update
                if chunk + 1 < chunks and sub == pieces - 2:
                    following = spread_turns(chunk + 1)
            turns = following
        last = contract_chunk(chunks - 1)
        final = (acc[...] + last).astype(BF16)

        @pl.when(step == 0)
        def _():
            pl.semaphore_wait(barrier, owners - 1 + peers - 1)

        for side_of in range(2):
            group = 2 * chip + side_of
            piece = final[side_of * GB : (side_of + 1) * GB]

            @pl.when(group != me_d)
            def _():
                models_out[group, span, :] = piece
                models_copy(group, me_d, part, group).start()

            @pl.when(group == me_d)
            def _():
                models_in[me_d, span, :] = piece

        return carry

    lax.fori_loop(0, pairs * gain_blocks, predict_step, 0)
    for fetch in fetches[6:]:
        fetch.wait()


    ridge = jnp.broadcast_to(ridge_ref[...], (8, columns))
    lane = lax.broadcasted_iota(jnp.int32, (8, columns), 1)
    reach = 2 * (ITERS - 1)

    def over_rows(value):
        total = jnp.sum(jnp.sum(value, axis=0), axis=0, keepdims=True)
        return jnp.broadcast_to(total, (8, columns))

    def moved(value, far):
        rolled = {0: value}
        for shift in range(2, far + 1, 2):
            rolled[shift] = pltpu.roll(value, columns - shift, 1)
            rolled[-shift] = pltpu.roll(value, shift, 1)
        out = {0: value}
        for shift in range(2, far + 1, 2):
            right, left = rolled[shift], rolled[-shift]
            for step in range(shift // 2):
                mirror = shift - 2 - 4 * step
                left = jnp.where(lane // 2 == step, rolled[mirror], left)
                right = jnp.where(lane // 2 == columns // 2 - 1 - step, rolled[-mirror], right)
            out[shift], out[-shift] = right, left
        return out

    def sweep_gain(constant, couple):
        base = moved(constant, reach)
        gain = {shift: base[shift] + 2.0 * couple[shift] for shift in base}
        for sweep in range(1, ITERS):
            far = reach - 2 * sweep
            gain = {
                shift: base[shift] + couple[shift] * (gain[shift - 2] + gain[shift + 2])
                for shift in range(-far, far + 1, 2)
            }
        return gain[0]

    per_gain = GB // BB

    def peel_owner(part, owner, rest):
        models = [
            models_in[
                owner,
                part * GB : (part + 1) * GB,
                position * columns : (position + 1) * columns,
            ]
            .astype(F32)
            .reshape(GB // 8, 8, columns)
            for position in range(DIR_DEV)
        ]
        gains = []
        for position in range(DIR_DEV):
            model = models[position]
            inverse = 1.0 / (over_rows(model * model) + ridge)
            couple = moved(0.5 * ridge * inverse, reach)
            cross_sum = over_rows(rest * model)
            for before in range(position):
                cross_sum = cross_sum - gains[before] * over_rows(models[before] * model)
            gains.append(sweep_gain(cross_sum * inverse, couple))
        for position in range(DIR_DEV):
            rest = rest - gains[position][None] * models[position]
        return rest.astype(BF16).astype(F32)

    def resid_copy(group, part, sem, to):
        span = pl.ds(group * group_blocks + part * per_gain, per_gain)
        return pltpu.make_async_remote_copy(
            src_ref=resid.at[span],
            dst_ref=resid.at[span],
            send_sem=r_send.at[part, sem],
            recv_sem=r_recv.at[part, group],
            device_id={"dir": to},
            device_id_type=MESH,
        )

    for part in range(gain_blocks):
        for k in range(1, owners):
            source = lax.rem(me_d + k, owners)
            models_copy(source, source, part, source).wait()
        rest = (
            vis_buf[part * GB : (part + 1) * GB, :].astype(F32).reshape(GB // 8, 8, columns)
        )
        for owner in range(owners):
            rest = peel_owner(part, owner, rest)
        resid[pl.ds(me_d * group_blocks + part * per_gain, per_gain)] = rest.reshape(
            per_gain, BB, columns
        ).astype(BF16)
        for k in range(1, owners):
            to = lax.rem(me_d + k, owners)
            resid_copy(me_d, part, to, to).start()
    resid[block_count] = jnp.zeros((BB, columns), BF16)

    slot_lanes = block_row.shape[1]
    tiles = jnp.broadcast_to(tile_ref[...], (slot_lanes, block_count))
    named_tile = jnp.where(
        lax.broadcasted_iota(jnp.int32, (slot_lanes, block_count), 0) == tiles, 1.0, 0.0
    )
    earlier = jnp.where(
        lax.broadcasted_iota(jnp.int32, (block_count, block_count), 0)
        < lax.broadcasted_iota(jnp.int32, (block_count, block_count), 1),
        1.0,
        0.0,
    )
    ranks = jnp.dot(named_tile.astype(BF16), earlier.astype(BF16), preferred_element_type=F32)
    slot = jnp.sum(ranks * named_tile, axis=0, keepdims=True).astype(jnp.int32)
    target = jnp.broadcast_to(tile_ref[...] * slots + slot, (slot_lanes, block_count))
    lane = lax.broadcasted_iota(jnp.int32, (slot_lanes, block_count), 0)
    taken = jnp.where(lane == target, 1.0, 0.0).astype(BF16)
    block_id = lax.broadcasted_iota(jnp.int32, (8, block_count), 1) - block_count
    picked = lax.dot_general(
        block_id.astype(F32).astype(BF16),
        taken,
        (((1,), (1,)), ((), ())),
        preferred_element_type=F32,
    )
    block_row[...] = picked[0:1, :].astype(jnp.int32) + block_count
    index_copy = pltpu.make_async_copy(block_row, block_of_ref, local_sem.at[len(fetches)])
    index_copy.start()

    in_block = (
        lax.broadcasted_iota(jnp.int32, (block_count, sample_rows), 1) // BB
        == lax.broadcasted_iota(jnp.int32, (block_count, sample_rows), 0)
    )
    at_lane = jnp.where(
        lax.broadcasted_iota(jnp.int32, (sample_rows, LANES), 0) % BB
        == lax.broadcasted_iota(jnp.int32, (sample_rows, LANES), 1) % BB,
        1.0,
        0.0,
    ).astype(BF16)
    packed, side = coords_out.shape[1], coords_out.shape[1] // 2
    spot = lax.broadcasted_iota(jnp.int32, (peers * packed, block_count), 0)
    place_of = tile_ref[...] * packed + slot
    sent = jnp.zeros((peers * packed, LANES), F32)
    for which, row in enumerate((u_row, v_row)):
        spread = jnp.where(in_block, jnp.broadcast_to(row, in_block.shape), 0.0).astype(BF16)
        by_block = jnp.dot(spread, at_lane, preferred_element_type=F32).astype(BF16)
        chosen = jnp.where(spot == place_of + which * side, 1.0, 0.0).astype(BF16)
        sent = sent + jnp.dot(chosen, by_block, preferred_element_type=F32)
    coords_out[...] = sent.astype(BF16).reshape(peers, packed, LANES)

    lax.fori_loop(1, peers, send_coords, 0)
    coords_in[me_t] = coords_out[me_t]
    index_copy.wait()

    for part in range(gain_blocks):
        for k in range(1, owners):
            source = lax.rem(me_d + k, owners)
            resid_copy(source, part, source, source).wait_recv()

    def block_in(to, slot):
        block = block_of_ref[0, to * slots + slot]
        return jnp.minimum(jnp.maximum(block, 0), block_count)

    def half_of(which):
        return pl.ds(pl.multiple_of(which * half_rows, half_rows), half_rows)

    def rows_copy(src, owner, to):
        return pltpu.make_async_remote_copy(
            src_ref=rows_out.at[src],
            dst_ref=rows_in.at[owner, half_of(core)],
            send_sem=d_send.at[src],
            recv_sem=d_recv.at[owner],
            device_id={"tb": to},
            device_id_type=MESH,
        )

    def hand_over(owner, which):
        return pltpu.make_async_remote_copy(
            src_ref=rows_in.at[owner, half_of(which)],
            dst_ref=rows_in.at[owner, half_of(which)],
            send_sem=f_send.at[owner],
            recv_sem=f_recv.at[owner],
            device_id={"dir": partner},
            device_id_type=MESH,
        )

    def paired(k):
        other, bit = 0, 1
        while bit < peers:
            other = other + bit * ((me_t // bit + k // bit) % 2)
            bit = 2 * bit
        return other

    def dispatch(k, carry):
        to = lax.rem(me_t + k, peers)
        for slot in range(half_slots):
            rows_out[to, slot * BB : (slot + 1) * BB, :] = resid[
                block_in(to, core * half_slots + slot)
            ]
        rows_copy(to, me_t, to).start()
        return carry

    lax.fori_loop(1, peers, dispatch, 0)
    for slot in range(slots):
        own_rows[slot * BB : (slot + 1) * BB, :] = resid[block_in(me_t, slot)]
    resid_ref[...] = resid[0:block_count].reshape(sample_rows, columns)

    def wait_coords(k, carry):
        source = lax.rem(me_t + k, peers)
        coords_copy(source, source, source).wait()
        return carry

    lax.fori_loop(1, peers, wait_coords, 0)
    share = grid_ref.shape[1]
    lines = share // GRID
    slots_wide = LANES // BB
    strips_wide = -(-slot_rows // LANES)
    wide = strips_wide * LANES
    x_of = (
        me_d * lines - GRID // 2 + lax.broadcasted_iota(jnp.int32, (lines, wide), 0)
    ).astype(F32) / (2.0 * GRID)
    y_of = (lax.broadcasted_iota(jnp.int32, (GRID, wide), 0) - GRID // 2).astype(F32) / (
        2.0 * GRID
    )
    slot_at = lax.broadcasted_iota(jnp.int32, (side, LANES), 0)
    slot_for = lax.broadcasted_iota(jnp.int32, (side, LANES), 1) // BB

    def make_table(source, carry):
        given = coords_in[source].astype(F32)

        def flat(rows):
            return jnp.concatenate(
                [
                    jnp.sum(
                        jnp.where(slot_at == slot_for + strip * slots_wide, rows, 0.0),
                        axis=0,
                        keepdims=True,
                    )
                    for strip in range(strips_wide)
                ],
                axis=1,
            )

        cos_x, sin_x = turn_cos_sin(x_of * flat(given[0:side]))
        cos_y, sin_y = turn_cos_sin(y_of * flat(given[side:packed]))
        for line in range(lines):
            cos_l, sin_l = cos_x[line : line + 1], sin_x[line : line + 1]
            rows = slice(line * GRID, (line + 1) * GRID)
            lower = slice(share + line * GRID, share + (line + 1) * GRID)
            cos_part = (cos_l * cos_y - sin_l * sin_y).astype(BF16)
            sin_part = (sin_l * cos_y + cos_l * sin_y).astype(BF16)
            tables[source, rows, :] = cos_part[:, 0:slot_rows]
            tables[source, lower, :] = sin_part[:, 0:slot_rows]
        return carry

    lax.fori_loop(0, peers, make_table, 0)

    grid_sum = jnp.dot(tables[me_t], own_rows[...], preferred_element_type=F32)

    def source_at(k):
        return paired(k)

    def arrive(k):
        source = source_at(k)
        rows_copy(source, source, source).wait_recv()
        hand_over(source, core).start()

    def add_source(k, total):
        @pl.when(k + 4 < peers)
        def _():
            arrive(k + 4)

        source = source_at(k)
        hand_over(source, 1 - core).wait_recv()
        return total + jnp.dot(tables[source], rows_in[source], preferred_element_type=F32)

    for ahead in range(1, min(4, peers - 1) + 1):
        arrive(ahead)
    grid_sum = lax.fori_loop(1, peers, add_source, grid_sum)
    grid_ref[...] = (grid_sum * float(ROWS_DEV) ** (-0.5)).reshape(2, share, columns)

    for part in range(gain_blocks):
        for k in range(1, owners):
            to = lax.rem(me_d + k, owners)
            resid_copy(me_d, part, to, to).wait_send()

    def drain(k, carry):
        to = lax.rem(me_t + k, peers)
        rows_copy(to, me_t, to).wait_send()
        hand_over(to, core).wait_send()
        return carry

    lax.fori_loop(1, peers, drain, 0)


def finish(resid_ref, grid_ref, resid_out, grid_out, sem):
    copies = (
        pltpu.make_async_copy(resid_ref, resid_out, sem.at[0]),
        pltpu.make_async_copy(grid_ref, grid_out, sem.at[1]),
    )
    for copy in copies:
        copy.start()
    for copy in copies:
        copy.wait()


def local(
    owners,
    peers,
    visibilities,
    uv_coords,
    comp_lm,
    spectra,
    ridge_weight,
    assignment,
    peel_order,
    block_tile,
):
    sample_rows, columns = visibilities.shape
    comps = comp_lm.shape[1]
    block_count = sample_rows // BB
    slots = max(2, 2 * block_count // peers)
    share = PIX // owners

    slot_lanes = -(-peers * slots // LANES) * LANES
    packed = 16 * -(-slots // 8)
    group_rows = sample_rows // owners
    half_rows = slots // 2 * BB
    vmem = pl.BlockSpec(memory_space=pltpu.VMEM)
    anywhere = pl.BlockSpec(memory_space=pl.ANY)
    dma = pltpu.SemaphoreType.DMA
    residual, subgrid = pl.pallas_call(
        functools.partial(kernel, owners, peers, slots),
        out_shape=(
            pltpu.VMEM((sample_rows, columns), BF16),
            pltpu.VMEM((2, share, columns), F32),
        ),
        in_specs=[anywhere] * 8,
        out_specs=(vmem, vmem),
        scratch_shapes=[
            pltpu.VMEM((2, comps), F32),
            pltpu.VMEM((comps // LANES, LANES), jnp.int32),
            pltpu.SMEM((DIR_DEV,), jnp.int32),
            pltpu.VMEM((2, sample_rows), BF16),
            pltpu.VMEM((comps, 2 * columns), BF16),
            pltpu.VMEM((group_rows, columns), BF16),
            pltpu.VMEM((1, columns), F32),
            pltpu.VMEM((1, block_count), jnp.int32),
            pltpu.VMEM((comps, 2 * DIR_DEV * columns), BF16),
            pltpu.VMEM((8, comps), BF16),
            pltpu.VMEM((sample_rows, 8), BF16),
            pltpu.VMEM((1, slot_lanes), jnp.int32),
            pltpu.SMEM((1, slot_lanes), jnp.int32),
            pltpu.VMEM((peers, packed, LANES), BF16),
            pltpu.VMEM((2 * GB, 2 * CHUNK), BF16),
            pltpu.VMEM((2 * GB, 2 * CHUNK), BF16),
            pltpu.VMEM((2 * GB, DIR_DEV * columns), F32),
            pltpu.VMEM((owners, group_rows, DIR_DEV * columns), BF16),
            pltpu.VMEM((owners, group_rows, DIR_DEV * columns), BF16),
            pltpu.VMEM((block_count + 1, BB, columns), BF16),
            pltpu.VMEM((slots * BB, columns), BF16),
            pltpu.VMEM((peers, half_rows, columns), BF16),
            pltpu.VMEM((peers, slots * BB, columns), BF16),
            pltpu.VMEM((peers, packed, LANES), BF16),
            pltpu.VMEM((peers, 2 * share, slots * BB), BF16),
            dma((group_rows // GB, owners)),
            dma((group_rows // GB, owners)),
            dma((group_rows // GB, owners)),
            dma((group_rows // GB, owners)),
            dma((peers,)),
            dma((peers,)),
            dma((peers,)),
            dma((peers,)),
            dma((peers,)),
            dma((peers,)),
            dma((10,)),
        ],
        compiler_params=pltpu.CompilerParams(
            collective_id=0, has_side_effects=True, vmem_limit_bytes=60 * 1024 * 1024
        ),
    )(
        comp_lm,
        assignment.reshape(comps // LANES, LANES),
        peel_order,
        uv_coords,
        spectra,
        visibilities,
        ridge_weight[None, :],
        block_tile.reshape(1, block_count),
    )
    residual, subgrid = pl.pallas_call(
        finish,
        out_shape=(
            jax.ShapeDtypeStruct(residual.shape, residual.dtype),
            jax.ShapeDtypeStruct(subgrid.shape, subgrid.dtype),
        ),
        in_specs=[vmem] * 2,
        out_specs=(anywhere, anywhere),
        scratch_shapes=[dma((2,))],
    )(
        pltpu.with_memory_space_constraint(residual, pltpu.VMEM),
        pltpu.with_memory_space_constraint(subgrid, pltpu.VMEM),
    )
    return residual, subgrid[None]


def solution(mesh):
    return jax.shard_map(
        functools.partial(local, mesh.shape["dir"], mesh.shape["tb"]),
        mesh=mesh,
        in_specs=(
            P("tb", None),
            P(None, "tb"),
            P(None, "dir"),
            P(None, "dir", None),
            P(),
            P("dir"),
            P("dir"),
            P("tb", None),
        ),
        out_specs=(P("tb", None), P("tb", None, "dir", None)),
        check_vma=False,
    )
```
